32 devices in a mesh: groups: 2 (over y), tm: 16 (over z, x, core).
Axes of the slice: x: 2, y: 2, z: 4, core: 2. Of those that a mesh axis runs over, the one named last changes fastest.
Arguments:
- positions: float32 [128, 3, 1536], P(('groups', 'tm')), parts along dimension 0, may hold values from -6 to 6
- atom_pairs: int32 [2, 8192], replicated, may hold values from 0 to 1535, as said below
- frame_counts: int32 [32], P('groups'), parts along dimension 0, may hold values from 1 to 4, as said below
Outputs:
- mean_now: float32 [16384], P('groups'), parts along dimension 0
- mean_lag: float32 [16384], P('groups'), parts along dimension 0
- cov_now: float32 [16384, 8192], P(('groups', 'tm')), parts along dimension 0
- cov_lag: float32 [16384, 8192], P(('groups', 'tm')), parts along dimension 0
The draws below stay inside these ranges and needn't reach their ends.
There are 2 independent parts, one for each index of `groups`. The reference program is written for one: setup_inputs(seed, part) draws one part's arguments, and reference() takes and returns one part's arrays. A program takes and returns all parts, laid end to end along the dimension named above; an argument that names none is the same for every part. Nothing has to cross between parts.
Inputs may be any that keep to these rules, and one draw needn't show every extreme that they name: `atom_pairs`: the two atoms of a pair differ; every atom is the first atom of some pair. Each block's valid frames are its first frame_counts frames; in every draw one block holds 4 valid frames and another 1.
All inputs are finite; a program needn't handle non-finite values.
Results may differ from the reference program's by a relative error of at most 0.0029.
Values sent between devices are 32-bit elements; how exact they have to be, the bound alone decides.
A program may use at most 192 MiB of HBM per device.

```python
import jax
import jax.numpy as jnp
from jax import lax

PAIRS = 8192
ATOMS = 1536
FR = 4
LAG = 1
BLOCKS = 16
TOTAL = 64


def draw_positions(key, part):
    keys = jax.random.split(key, 5)
    frame_index = jnp.arange(TOTAL, dtype=jnp.float32)[:, None, None]
    base = 1.5 * jax.random.truncated_normal(keys[0], -3.0, 3.0, (1, 3, ATOMS), jnp.float32)
    period = jnp.exp(jax.random.uniform(keys[1], (1, 3, ATOMS), jnp.float32, minval=jnp.log(4.0 * LAG), maxval=jnp.log(4.0 * TOTAL)))
    phase = jax.random.uniform(keys[2], (1, 3, ATOMS), jnp.float32, minval=-3.14159, maxval=3.14159)
    amplitude = jax.random.uniform(keys[3], (1, 3, ATOMS), jnp.float32, minval=0.2, maxval=0.6)
    noise = 0.15 * jax.random.truncated_normal(keys[4], -3.0, 3.0, (TOTAL, 3, ATOMS), jnp.float32)
    wave = jnp.sin(6.2831853 * frame_index / period + phase)
    return (base + amplitude * wave + noise).astype(jnp.float32)


def draw_atom_pairs(key, part):
    keys = jax.random.split(key, 2)
    ordering = jax.random.permutation(keys[0], ATOMS).astype(jnp.int32)
    first_atom = ordering[jnp.arange(PAIRS, dtype=jnp.int32) % ATOMS]
    offsets = jax.random.randint(keys[1], (PAIRS,), 1, ATOMS, dtype=jnp.int32)
    second_atom = (first_atom + offsets) % ATOMS
    return jnp.stack([first_atom, second_atom]).astype(jnp.int32)


def draw_frame_counts(key, part):
    keys = jax.random.split(key, 3)
    lowest = FR // 4
    counts = jax.random.randint(keys[0], (BLOCKS,), lowest, FR + 1, dtype=jnp.int32)
    full_block = jax.random.randint(keys[1], (), 0, BLOCKS, dtype=jnp.int32)
    short_block = (full_block + jax.random.randint(keys[2], (), 1, BLOCKS, dtype=jnp.int32)) % BLOCKS
    counts = counts.at[full_block].set(FR)
    counts = counts.at[short_block].set(lowest)
    return counts.astype(jnp.int32)


def setup_inputs(seed: int = 0, part: int = 0) -> dict:
    key_of = jax.random.split(jax.random.key(seed), 4)
    own_keys = jax.random.split(jax.random.fold_in(key_of[3], part), 4)
    positions = draw_positions(jax.random.fold_in(jax.random.fold_in(key_of[3], part), 71), part)
    atom_pairs = draw_atom_pairs(jax.random.fold_in(key_of[3], 71), part)
    frame_counts = draw_frame_counts(jax.random.fold_in(jax.random.fold_in(key_of[3], part), 71), part)
    return dict(positions=positions, atom_pairs=atom_pairs, frame_counts=frame_counts)


def featurize(frames, atom_pairs):
    first_atom = jnp.take(frames, atom_pairs[0], axis=2)
    second_atom = jnp.take(frames, atom_pairs[1], axis=2)
    difference = first_atom - second_atom
    return jnp.sqrt(lax.optimization_barrier(jnp.sum(difference * difference, axis=1)))

def reference(positions, atom_pairs, frame_counts):
    total = positions.shape[0]
    frame_index = jnp.arange(total, dtype=jnp.int32)
    block_of = (frame_index // FR).astype(jnp.int32)
    valid = frame_index % FR < frame_counts[block_of]
    valid_ahead = jnp.concatenate([valid[LAG:], jnp.zeros((LAG,), dtype=bool)])
    weights = (valid & valid_ahead).astype(jnp.float32)
    pair_count = jnp.sum(weights)
    features = featurize(positions, atom_pairs)
    ahead = jnp.concatenate([features[LAG:], jnp.zeros((LAG, features.shape[1]), jnp.float32)], axis=0)
    mean_now = lax.optimization_barrier(jnp.sum(weights[:, None] * features, axis=0)) / pair_count
    mean_lag = lax.optimization_barrier(jnp.sum(weights[:, None] * ahead, axis=0)) / pair_count
    early = lax.optimization_barrier((features - mean_now).astype(jnp.bfloat16)).astype(jnp.float32)
    late = lax.optimization_barrier((ahead - mean_lag).astype(jnp.bfloat16)).astype(jnp.float32)
    weighted = early * weights[:, None]
    cov_now = jnp.dot(weighted.T, early, preferred_element_type=jnp.float32, precision=lax.Precision.HIGHEST) / pair_count
    cov_lag = jnp.dot(weighted.T, late, preferred_element_type=jnp.float32, precision=lax.Precision.HIGHEST) / pair_count
    return (mean_now, mean_lag, cov_now, cov_lag)
```

```python
import functools

import jax
import jax.numpy as jnp
from jax import lax
from jax.experimental import pallas as pl
from jax.experimental.pallas import tpu as pltpu
from jax.sharding import PartitionSpec as P

FR = 4
LAG = 1
CORES = 2
PIECES = 2
MIB = 1024 * 1024


def axis_split(devices):
    chips = devices // CORES
    x = 1
    while x * x * x * 8 <= chips and chips % (x * 2) == 0:
        x *= 2
    return chips // x, x


def scoped(devices, wide):
    return (24 if devices <= 32 else wide) * MIB


def split_rows(values):
    parts = []
    for _ in range(PIECES):
        part = values.astype(jnp.bfloat16)
        parts.append(part)
        values = values - part.astype(jnp.float32)
    return parts


def split_into(split_ref, blocks_ref, first):
    frames = split_ref.shape[0] // (3 * PIECES)
    atoms = split_ref.shape[1]
    group = min(frames, 32)

    def split_group(g, carry):
        blocks = blocks_ref[pl.ds(first + g * (group // FR), group // FR)]
        for c in range(3):
            values = blocks[:, c, :, :].reshape(group, atoms)
            for s, part in enumerate(split_rows(values)):
                row = (3 * s + c) * frames + g * group
                if frames != group:
                    row = pl.multiple_of(row, group)
                split_ref[pl.ds(row, group), :] = part
        return carry

    if frames == group:
        split_group(0, 0)
    else:
        lax.fori_loop(0, frames // group, split_group, 0)


def distances(split, select):
    parts = jnp.dot(split, select, preferred_element_type=jnp.float32)
    rows = parts.shape[0] // PIECES
    frames = rows // 3
    difference = parts[:rows]
    for s in range(1, PIECES):
        difference = difference + parts[s * rows : (s + 1) * rows]
    squares = difference * difference
    return jnp.sqrt(squares[:frames] + squares[frames : 2 * frames] + squares[2 * frames :])


def ahead_of(rows):
    return jnp.concatenate([rows[LAG:], jnp.zeros((LAG, rows.shape[1]), rows.dtype)], axis=0)


def exchange_kernel(
    sizes,
    own_ref,
    pairs_hbm,
    counts_hbm,
    blocks_ref,
    select_ref,
    half_ref,
    weights_ref,
    pairs_ref,
    counts_ref,
    split_ref,
    load_sem,
    send_sem,
    recv_sem,
    share_sem,
    fetch_sem,
):
    zs, xs = sizes
    me = lax.axis_index("tm")
    core = lax.rem(me, CORES)
    x = lax.rem(me // CORES, xs)
    z = me // (CORES * xs)
    chunks, atoms, width = select_ref.shape
    frames = blocks_ref.shape[0] * FR

    def index(zi, xi, ci):
        return (zi * xs + xi) * CORES + ci

    def device(i):
        return {"tm": i}

    loads = [
        pltpu.make_async_copy(pairs_hbm, pairs_ref, load_sem.at[0]),
        pltpu.make_async_copy(own_ref, blocks_ref.at[me], load_sem.at[1]),
        pltpu.make_async_copy(counts_hbm, counts_ref, load_sem.at[2]),
    ]
    for load in loads:
        load.start()

    sibling = index(z, x, 1 - core)
    x_peers = [lax.rem(x + d, xs) for d in range(1, xs)]
    z_peers = [lax.rem(z + d, zs) for d in range(1, zs)]
    barrier = pltpu.get_barrier_semaphore()

    def greet(i):
        pl.semaphore_signal(
            barrier, inc=1, device_id=device(i), device_id_type=pl.DeviceIdType.MESH
        )

    for p in z_peers:
        greet(index(p, x, core))
    for p in x_peers:
        greet(index(z, p, core))
    greet(sibling)

    def build_select(j, carry):
        atom = lax.broadcasted_iota(jnp.int32, (atoms, width), 0).astype(jnp.int16)
        start = pl.multiple_of(j * width, width)
        first = pairs_ref[0:1, pl.ds(start, width)].astype(jnp.int16)
        second = pairs_ref[1:2, pl.ds(start, width)].astype(jnp.int16)
        one, zero = jnp.bfloat16(1.0), jnp.bfloat16(0.0)
        select_ref[j] = jnp.where(atom == first, one, jnp.where(atom == second, -one, zero))
        return carry

    marks = [chunks * p // 16 for p in BUILD]
    done = [0]

    def build_to(mark):
        if mark > done[0]:
            lax.fori_loop(done[0], mark, build_select, 0)
            done[0] = mark

    loads[0].wait()
    build_to(marks[0])
    pl.semaphore_wait(barrier, len(z_peers) + len(x_peers) + 1)

    sent = []

    def send(source, block, target, allowed):
        copy = pltpu.make_async_remote_copy(
            src_ref=source,
            dst_ref=blocks_ref.at[block],
            send_sem=send_sem.at[len(sent)],
            recv_sem=recv_sem.at[block],
            device_id=device(target),
            device_id_type=pl.DeviceIdType.MESH,
        )
        sent.append((copy, allowed))
        if allowed is None:
            copy.start()
        else:
            pl.when(allowed)(copy.start)

    def arrived(block):
        pltpu.make_async_remote_copy(
            src_ref=blocks_ref.at[block],
            dst_ref=blocks_ref.at[block],
            send_sem=send_sem.at[0],
            recv_sem=recv_sem.at[block],
            device_id=device(sibling),
            device_id_type=pl.DeviceIdType.MESH,
        ).wait_recv()

    for p in x_peers:
        send(own_ref, me, index(z, p, core), None)
    for d in range(1, zs):
        for sign in (1, -1):
            target = z + sign * d
            exists = target < zs if sign > 0 else target >= 0
            send(own_ref, me, index(target, x, core), exists)
    send(own_ref, me, sibling, None)

    def origins(d):
        for sign in (-1, 1) if d else (1,):
            origin = z + sign * d
            yield origin, None if d == 0 else (origin >= 0 if sign < 0 else origin < zs)

    def z_event(d):
        for origin, exists in origins(d):
            block = index(origin, x, core)
            pl.when(exists)(functools.partial(arrived, block))
            for p in x_peers:
                send(blocks_ref.at[block], block, index(z, p, core), exists)
            send(blocks_ref.at[block], block, sibling, exists)

    def x_event(d):
        for origin, exists in origins(d):
            for p in x_peers:
                block = index(origin, p, core)
                if exists is None:
                    arrived(block)
                else:
                    pl.when(exists)(functools.partial(arrived, block))
                send(blocks_ref.at[block], block, sibling, exists)

    near = zs // 2
    events = [functools.partial(z_event, 1)]
    for d in range(1, zs):
        if d + 1 < zs:
            events.append(functools.partial(z_event, d + 1))
        events.append(functools.partial(x_event, d - 1))
        if d == near:
            early = len(events)
    events.append(functools.partial(x_event, zs - 1))

    build_to(marks[1])
    for loads_left in loads[1:]:
        loads_left.wait()
    frame = lax.broadcasted_iota(jnp.int32, (frames, 128), 0)

    def add_block(b, current):
        return jnp.where(frame // FR == b, counts_ref[b], current)

    current = lax.fori_loop(0, frames // FR, add_block, jnp.zeros((frames, 128), jnp.int32))
    valid = jnp.where(frame % FR < current, 1.0, 0.0)
    weights_ref[...] = valid * ahead_of(valid)
    for e, event in enumerate(events[:early]):
        event()
        build_to(marks[min(e + 2, len(marks) - 1)])
    build_to(chunks)

    half = z // near
    for zi in range(near):
        for xi in range(xs):
            arrived(index(half * near + zi, xi, 1 - core))
    count = near * xs * CORES
    split_into(split_ref, blocks_ref, half * count)

    def share(j):
        return pltpu.make_async_remote_copy(
            src_ref=half_ref.at[j],
            dst_ref=half_ref.at[j],
            send_sem=share_sem.at[j],
            recv_sem=fetch_sem.at[j],
            device_id=device(sibling),
            device_id_type=pl.DeviceIdType.MESH,
        )

    per_core = chunks // CORES
    first_chunk = core * per_core

    def featurize(i, carry):
        j = first_chunk + i
        half_ref[j] = distances(split_ref[...], select_ref[j])
        share(j).start()
        return carry

    late = events[early:]
    for k in range(len(late) + 1):
        lax.fori_loop(
            per_core * k // (len(late) + 1),
            per_core * (k + 1) // (len(late) + 1),
            featurize,
            0,
        )
        if k < len(late):
            late[k]()

    for zi in range(near):
        for xi in range(xs):
            arrived(index((1 - half) * near + zi, xi, 1 - core))

    def finish(i, carry):
        share(first_chunk + i).wait_send()
        share((1 - core) * per_core + i).wait_recv()
        return carry

    lax.fori_loop(0, per_core, finish, 0)
    for copy, allowed in sent:
        if allowed is None:
            copy.wait_send()
        else:
            pl.when(allowed)(copy.wait_send)


BUILD = [3, 11, 12, 13, 14, 15, 16]


def exchange(block, atom_pairs, frame_counts, devices, chunk):
    zs, xs = axis_split(devices)
    atoms = block.shape[2]
    frames = devices * FR
    chunks = atom_pairs.shape[1] // chunk
    dma = pltpu.SemaphoreType.DMA
    sends = (xs - 1) + 2 * (zs - 1) + 1 + 2 * (zs - 1) * xs + (2 * zs - 1) * (xs - 1)
    return pl.pallas_call(
        functools.partial(exchange_kernel, (zs, xs)),
        out_shape=(
            pltpu.VMEM((devices,) + block.shape, jnp.float32),
            pltpu.VMEM((chunks, atoms, chunk), jnp.bfloat16),
            pltpu.VMEM((chunks, frames // 2, chunk), jnp.float32),
            pltpu.VMEM((frames, 128), jnp.float32),
        ),
        in_specs=[pl.BlockSpec(memory_space=pltpu.HBM)] * 3,
        out_specs=(pl.BlockSpec(memory_space=pltpu.VMEM),) * 4,
        scratch_shapes=[
            pltpu.VMEM(atom_pairs.shape, jnp.int32),
            pltpu.SMEM(frame_counts.shape, jnp.int32),
            pltpu.VMEM((3 * PIECES * frames // 2, atoms), jnp.bfloat16),
            dma((3,)),
            dma((sends,)),
            dma((devices,)),
            dma((chunks,)),
            dma((chunks,)),
        ],
        compiler_params=pltpu.CompilerParams(
            collective_id=0, has_side_effects=True, vmem_limit_bytes=scoped(devices, 14)
        ),
        name="exchange",
    )(*(pltpu.with_memory_space_constraint(a, pltpu.HBM) for a in (block, atom_pairs, frame_counts)))


def covariance_kernel(
    row_count,
    blocks_ref,
    select_ref,
    half_ref,
    weights_ref,
    mean_now_ref,
    mean_lag_ref,
    cov_now_ref,
    cov_lag_ref,
    left_ref,
    split_ref,
    features_ref,
):
    step = pl.program_id(0)
    steps = pl.num_programs(0)
    chunks, part, width = half_ref.shape
    me = lax.axis_index("tm")
    held = blocks_ref.shape[0]
    mine = me // (held // 2)
    other = 1 - mine
    first = me * row_count // width

    def widened(rows):
        return jnp.concatenate([rows] * (width // 128), axis=1)

    def factor():
        return widened(1.0 / jnp.sum(weights_ref[...], axis=0, keepdims=True))

    def mean_of(rows):
        return jnp.sum(widened(weights_ref[...]) * rows, axis=0, keepdims=True) * factor()

    def next_features(s):
        j = lax.rem(first + s, chunks)
        features_ref[pl.ds(pl.multiple_of(mine * part, part), part), :] = half_ref[j]
        features_ref[pl.ds(pl.multiple_of(other * part, part), part), :] = distances(
            split_ref[...], select_ref[j]
        )

    @pl.when(step == 0)
    def _():
        split_into(split_ref, blocks_ref, other * (held // 2))
        next_features(0)
        features = features_ref[...]
        early = (features - mean_of(features)).astype(jnp.bfloat16).astype(jnp.float32)
        left = early * widened(weights_ref[...])
        left_ref[...] = jnp.transpose(left).astype(jnp.bfloat16)

    def outputs():
        features = features_ref[...]
        ahead = ahead_of(features)
        mean_now = mean_of(features)
        mean_lag = mean_of(ahead)
        mean_now_ref[...] = mean_now
        mean_lag_ref[...] = mean_lag
        early = (features - mean_now).astype(jnp.bfloat16)
        late = (ahead - mean_lag).astype(jnp.bfloat16)
        if row_count == width:
            left = left_ref[...]
        else:
            offset = lax.rem(me * row_count, width)
            left = left_ref[pl.ds(pl.multiple_of(offset, row_count), row_count), :]
        scale = factor()
        cov_now_ref[...] = jnp.dot(left, early, preferred_element_type=jnp.float32) * scale
        cov_lag_ref[...] = jnp.dot(left, late, preferred_element_type=jnp.float32) * scale

    @pl.when(step < steps - 1)
    def _():
        outputs()
        next_features(step + 1)

    @pl.when(step == steps - 1)
    def _():
        outputs()


def covariances(blocks, select, half, weights, row_count):
    chunks, part, chunk = half.shape
    atoms = blocks.shape[3]
    width = chunks * chunk
    row = jax.ShapeDtypeStruct((1, width), jnp.float32)
    matrix = jax.ShapeDtypeStruct((row_count, width), jnp.float32)

    def column(i):
        first = lax.axis_index("tm") * row_count // chunk
        return 0, lax.rem(first + i, chunks)

    return pl.pallas_call(
        functools.partial(covariance_kernel, row_count),
        out_shape=(row, row, matrix, matrix),
        grid=(chunks,),
        in_specs=[pl.BlockSpec(memory_space=pltpu.VMEM)] * 4,
        out_specs=(
            pl.BlockSpec((1, chunk), column),
            pl.BlockSpec((1, chunk), column),
            pl.BlockSpec((row_count, chunk), column),
            pl.BlockSpec((row_count, chunk), column),
        ),
        scratch_shapes=[
            pltpu.VMEM((chunk, 2 * part), jnp.bfloat16),
            pltpu.VMEM((3 * PIECES * part, atoms), jnp.bfloat16),
            pltpu.VMEM((2 * part, chunk), jnp.float32),
        ],
        compiler_params=pltpu.CompilerParams(vmem_limit_bytes=scoped(blocks.shape[0], 56)),
        name="covariances",
    )(blocks, select, half, weights)


def body(positions, atom_pairs, frame_counts):
    devices = lax.axis_size("tm")
    width = atom_pairs.shape[1]
    row_count = width // devices
    chunk = 512 if devices <= 32 else 128
    gathered = exchange(
        jnp.transpose(positions, (1, 0, 2)), atom_pairs, frame_counts, devices, chunk
    )
    mean_now, mean_lag, cov_now, cov_lag = covariances(*gathered, row_count)
    return (mean_now.reshape(width), mean_lag.reshape(width), cov_now, cov_lag)


def solution(mesh):
    return jax.shard_map(
        body,
        mesh=mesh,
        in_specs=(P(("groups", "tm"), None, None), P(), P("groups")),
        out_specs=(P("groups"), P("groups"), P(("groups", "tm"), None), P(("groups", "tm"), None)),
        check_vma=False,
    )
```

```python
import functools

import jax
import jax.numpy as jnp
from jax import lax
from jax.experimental import pallas as pl
from jax.experimental.pallas import tpu as pltpu
from jax.sharding import PartitionSpec as P

FR = 4
LAG = 1
CORES = 2
PIECES = 2
MIB = 1024 * 1024


def axis_split(devices):
    chips = devices // CORES
    x = 1
    while x * x * x * 8 <= chips and chips % (x * 2) == 0:
        x *= 2
    return chips // x, x


def scoped(devices, wide):
    return (24 if devices <= 32 else wide) * MIB


def split_rows(values):
    parts = []
    for _ in range(PIECES):
        part = values.astype(jnp.bfloat16)
        parts.append(part)
        values = values - part.astype(jnp.float32)
    return parts


def split_into(split_ref, blocks_ref, first):
    frames = split_ref.shape[0] // (3 * PIECES)
    atoms = split_ref.shape[1]
    group = min(frames, 32)

    def split_group(g, carry):
        blocks = blocks_ref[pl.ds(first + g * (group // FR), group // FR)]
        for c in range(3):
            values = blocks[:, c, :, :].reshape(group, atoms)
            for s, part in enumerate(split_rows(values)):
                row = (3 * s + c) * frames + g * group
                if frames != group:
                    row = pl.multiple_of(row, group)
                split_ref[pl.ds(row, group), :] = part
        return carry

    if frames == group:
        split_group(0, 0)
    else:
        lax.fori_loop(0, frames // group, split_group, 0)


def distances(split, select):
    parts = jnp.dot(split, select, preferred_element_type=jnp.float32)
    rows = parts.shape[0] // PIECES
    frames = rows // 3
    difference = parts[:rows]
    for s in range(1, PIECES):
        difference = difference + parts[s * rows : (s + 1) * rows]
    squares = difference * difference
    return jnp.sqrt(squares[:frames] + squares[frames : 2 * frames] + squares[2 * frames :])


def ahead_of(rows):
    return jnp.concatenate([rows[LAG:], jnp.zeros((LAG, rows.shape[1]), rows.dtype)], axis=0)


def exchange_kernel(
    sizes,
    own_ref,
    pairs_hbm,
    counts_hbm,
    blocks_ref,
    select_ref,
    half_ref,
    weights_ref,
    pairs_ref,
    counts_ref,
    split_ref,
    load_sem,
    send_sem,
    recv_sem,
    share_sem,
    fetch_sem,
):
    zs, xs = sizes
    me = lax.axis_index("tm")
    core = lax.rem(me, CORES)
    x = lax.rem(me // CORES, xs)
    z = me // (CORES * xs)
    chunks, atoms, width = select_ref.shape
    frames = blocks_ref.shape[0] * FR

    def index(zi, xi, ci):
        return (zi * xs + xi) * CORES + ci

    def device(i):
        return {"tm": i}

    loads = [
        pltpu.make_async_copy(pairs_hbm, pairs_ref, load_sem.at[0]),
        pltpu.make_async_copy(own_ref, blocks_ref.at[me], load_sem.at[1]),
        pltpu.make_async_copy(counts_hbm, counts_ref, load_sem.at[2]),
    ]
    for load in loads:
        load.start()

    sibling = index(z, x, 1 - core)
    x_peers = [lax.rem(x + d, xs) for d in range(1, xs)]
    z_peers = [lax.rem(z + d, zs) for d in range(1, zs)]
    barrier = pltpu.get_barrier_semaphore()

    def greet(i):
        pl.semaphore_signal(
            barrier, inc=1, device_id=device(i), device_id_type=pl.DeviceIdType.MESH
        )

    for p in z_peers:
        greet(index(p, x, core))
    for p in x_peers:
        greet(index(z, p, core))
    greet(sibling)

    def build_select(j, carry):
        atom = lax.broadcasted_iota(jnp.int32, (atoms, width), 0).astype(jnp.int16)
        start = pl.multiple_of(j * width, width)
        first = pairs_ref[0:1, pl.ds(start, width)].astype(jnp.int16)
        second = pairs_ref[1:2, pl.ds(start, width)].astype(jnp.int16)
        one, zero = jnp.bfloat16(1.0), jnp.bfloat16(0.0)
        select_ref[j] = jnp.where(atom == first, one, jnp.where(atom == second, -one, zero))
        return carry

    marks = [chunks * p // 16 for p in BUILD]
    done = [0]

    def build_to(mark):
        if mark > done[0]:
            lax.fori_loop(done[0], mark, build_select, 0)
            done[0] = mark

    loads[0].wait()
    build_to(marks[0])
    pl.semaphore_wait(barrier, len(z_peers) + len(x_peers) + 1)

    sent = []

    def send(source, block, target, allowed):
        copy = pltpu.make_async_remote_copy(
            src_ref=source,
            dst_ref=blocks_ref.at[block],
            send_sem=send_sem.at[len(sent)],
            recv_sem=recv_sem.at[block],
            device_id=device(target),
            device_id_type=pl.DeviceIdType.MESH,
        )
        sent.append((copy, allowed))
        if allowed is None:
            copy.start()
        else:
            pl.when(allowed)(copy.start)

    def arrived(block):
        pltpu.make_async_remote_copy(
            src_ref=blocks_ref.at[block],
            dst_ref=blocks_ref.at[block],
            send_sem=send_sem.at[0],
            recv_sem=recv_sem.at[block],
            device_id=device(sibling),
            device_id_type=pl.DeviceIdType.MESH,
        ).wait_recv()

    for p in x_peers:
        send(own_ref, me, index(z, p, core), None)
    for d in range(1, zs):
        for sign in (1, -1):
            target = z + sign * d
            exists = target < zs if sign > 0 else target >= 0
            send(own_ref, me, index(target, x, core), exists)
    send(own_ref, me, sibling, None)

    def origins(d):
        for sign in (-1, 1) if d else (1,):
            origin = z + sign * d
            yield origin, None if d == 0 else (origin >= 0 if sign < 0 else origin < zs)

    def z_event(d):
        for origin, exists in origins(d):
            block = index(origin, x, core)
            pl.when(exists)(functools.partial(arrived, block))
            for p in x_peers:
                send(blocks_ref.at[block], block, index(z, p, core), exists)
            send(blocks_ref.at[block], block, sibling, exists)

    def x_event(d):
        for origin, exists in origins(d):
            for p in x_peers:
                block = index(origin, p, core)
                if exists is None:
                    arrived(block)
                else:
                    pl.when(exists)(functools.partial(arrived, block))
                send(blocks_ref.at[block], block, sibling, exists)

    near = zs // 2
    events = [functools.partial(z_event, 1)]
    for d in range(1, zs):
        if d + 1 < zs:
            events.append(functools.partial(z_event, d + 1))
        events.append(functools.partial(x_event, d - 1))
        if d == near:
            early = len(events)
    events.append(functools.partial(x_event, zs - 1))

    build_to(marks[1])
    for loads_left in loads[1:]:
        loads_left.wait()
    frame = lax.broadcasted_iota(jnp.int32, (frames, 128), 0)

    def add_block(b, current):
        return jnp.where(frame // FR == b, counts_ref[b], current)

    current = lax.fori_loop(0, frames // FR, add_block, jnp.zeros((frames, 128), jnp.int32))
    valid = jnp.where(frame % FR < current, 1.0, 0.0)
    weights_ref[...] = valid * ahead_of(valid)
    for e, event in enumerate(events[:early]):
        event()
        build_to(marks[min(e + 2, len(marks) - 1)])
    build_to(chunks)

    half = z // near
    for zi in range(near):
        for xi in range(xs):
            arrived(index(half * near + zi, xi, 1 - core))
    count = near * xs * CORES
    split_into(split_ref, blocks_ref, half * count)

    def share(j):
        return pltpu.make_async_remote_copy(
            src_ref=half_ref.at[j],
            dst_ref=half_ref.at[j],
            send_sem=share_sem.at[j],
            recv_sem=fetch_sem.at[j],
            device_id=device(sibling),
            device_id_type=pl.DeviceIdType.MESH,
        )

    per_core = chunks // CORES
    first_chunk = core * per_core

    def featurize(i, carry):
        j = first_chunk + i
        half_ref[j] = distances(split_ref[...], select_ref[j])
        share(j).start()
        return carry

    late = events[early:]
    for k in range(len(late) + 1):
        lax.fori_loop(
            per_core * k // (len(late) + 1),
            per_core * (k + 1) // (len(late) + 1),
            featurize,
            0,
        )
        if k < len(late):
            late[k]()

    for zi in range(near):
        for xi in range(xs):
            arrived(index((1 - half) * near + zi, xi, 1 - core))

    def finish(i, carry):
        share(first_chunk + i).wait_send()
        share((1 - core) * per_core + i).wait_recv()
        return carry

    lax.fori_loop(0, per_core, finish, 0)
    for copy, allowed in sent:
        if allowed is None:
            copy.wait_send()
        else:
            pl.when(allowed)(copy.wait_send)


BUILD = [3, 11, 12, 13, 14, 15, 16]


def exchange(block, atom_pairs, frame_counts, devices, chunk):
    zs, xs = axis_split(devices)
    atoms = block.shape[2]
    frames = devices * FR
    chunks = atom_pairs.shape[1] // chunk
    dma = pltpu.SemaphoreType.DMA
    sends = (xs - 1) + 2 * (zs - 1) + 1 + 2 * (zs - 1) * xs + (2 * zs - 1) * (xs - 1)
    return pl.pallas_call(
        functools.partial(exchange_kernel, (zs, xs)),
        out_shape=(
            pltpu.VMEM((devices,) + block.shape, jnp.float32),
            pltpu.VMEM((chunks, atoms, chunk), jnp.bfloat16),
            pltpu.VMEM((chunks, frames // 2, chunk), jnp.float32),
            pltpu.VMEM((frames, 128), jnp.float32),
        ),
        in_specs=[pl.BlockSpec(memory_space=pltpu.HBM)] * 3,
        out_specs=(pl.BlockSpec(memory_space=pltpu.VMEM),) * 4,
        scratch_shapes=[
            pltpu.VMEM(atom_pairs.shape, jnp.int32),
            pltpu.SMEM(frame_counts.shape, jnp.int32),
            pltpu.VMEM((3 * PIECES * frames // 2, atoms), jnp.bfloat16),
            dma((3,)),
            dma((sends,)),
            dma((devices,)),
            dma((chunks,)),
            dma((chunks,)),
        ],
        compiler_params=pltpu.CompilerParams(
            collective_id=0, has_side_effects=True, vmem_limit_bytes=scoped(devices, 14)
        ),
        name="exchange",
    )(*(pltpu.with_memory_space_constraint(a, pltpu.HBM) for a in (block, atom_pairs, frame_counts)))


def covariance_kernel(
    row_count,
    blocks_ref,
    select_ref,
    half_ref,
    weights_ref,
    mean_now_ref,
    mean_lag_ref,
    cov_now_ref,
    cov_lag_ref,
    left_ref,
    split_ref,
    features_ref,
):
    step = pl.program_id(0)
    steps = pl.num_programs(0)
    chunks, part, width = half_ref.shape
    me = lax.axis_index("tm")
    held = blocks_ref.shape[0]
    mine = me // (held // 2)
    other = 1 - mine
    first = me * row_count // width

    def widened(rows):
        return jnp.concatenate([rows] * (width // 128), axis=1)

    def factor():
        return widened(1.0 / jnp.sum(weights_ref[...], axis=0, keepdims=True))

    def mean_of(rows):
        return jnp.sum(widened(weights_ref[...]) * rows, axis=0, keepdims=True) * factor()

    def next_features(s):
        j = lax.rem(first + s, chunks)
        slot = lax.rem(s, 2)
        features_ref[slot, pl.ds(pl.multiple_of(mine * part, part), part), :] = half_ref[j]
        features_ref[slot, pl.ds(pl.multiple_of(other * part, part), part), :] = distances(
            split_ref[...], select_ref[j]
        )

    @pl.when(step == 0)
    def _():
        split_into(split_ref, blocks_ref, other * (held // 2))
        next_features(0)
        features = features_ref[0]
        early = (features - mean_of(features)).astype(jnp.bfloat16).astype(jnp.float32)
        left = early * widened(weights_ref[...])
        left_ref[...] = jnp.transpose(left).astype(jnp.bfloat16)

    features = features_ref[lax.rem(step, 2)]
    ahead = ahead_of(features)
    mean_now = mean_of(features)
    mean_lag = mean_of(ahead)
    mean_now_ref[...] = mean_now
    mean_lag_ref[...] = mean_lag
    early = (features - mean_now).astype(jnp.bfloat16)
    late = (ahead - mean_lag).astype(jnp.bfloat16)
    if row_count == width:
        left = left_ref[...]
    else:
        offset = lax.rem(me * row_count, width)
        left = left_ref[pl.ds(pl.multiple_of(offset, row_count), row_count), :]
    scale = factor()
    cov_now_ref[...] = jnp.dot(left, early, preferred_element_type=jnp.float32) * scale
    cov_lag_ref[...] = jnp.dot(left, late, preferred_element_type=jnp.float32) * scale
    next_features(jnp.minimum(step + 1, steps - 1))


def covariances(blocks, select, half, weights, row_count):
    chunks, part, chunk = half.shape
    atoms = blocks.shape[3]
    width = chunks * chunk
    row = jax.ShapeDtypeStruct((1, width), jnp.float32)
    matrix = jax.ShapeDtypeStruct((row_count, width), jnp.float32)

    def column(i):
        first = lax.axis_index("tm") * row_count // chunk
        return 0, lax.rem(first + i, chunks)

    return pl.pallas_call(
        functools.partial(covariance_kernel, row_count),
        out_shape=(row, row, matrix, matrix),
        grid=(chunks,),
        in_specs=[pl.BlockSpec(memory_space=pltpu.VMEM)] * 4,
        out_specs=(
            pl.BlockSpec((1, chunk), column),
            pl.BlockSpec((1, chunk), column),
            pl.BlockSpec((row_count, chunk), column),
            pl.BlockSpec((row_count, chunk), column),
        ),
        scratch_shapes=[
            pltpu.VMEM((chunk, 2 * part), jnp.bfloat16),
            pltpu.VMEM((3 * PIECES * part, atoms), jnp.bfloat16),
            pltpu.VMEM((2, 2 * part, chunk), jnp.float32),
        ],
        compiler_params=pltpu.CompilerParams(vmem_limit_bytes=scoped(blocks.shape[0], 56)),
        name="covariances",
    )(blocks, select, half, weights)


def body(positions, atom_pairs, frame_counts):
    devices = lax.axis_size("tm")
    width = atom_pairs.shape[1]
    row_count = width // devices
    chunk = 512 if devices <= 32 else 128
    gathered = exchange(
        jnp.transpose(positions, (1, 0, 2)), atom_pairs, frame_counts, devices, chunk
    )
    mean_now, mean_lag, cov_now, cov_lag = covariances(*gathered, row_count)
    return (mean_now.reshape(width), mean_lag.reshape(width), cov_now, cov_lag)


def solution(mesh):
    return jax.shard_map(
        body,
        mesh=mesh,
        in_specs=(P(("groups", "tm"), None, None), P(), P("groups")),
        out_specs=(P("groups"), P("groups"), P(("groups", "tm"), None), P(("groups", "tm"), None)),
        check_vma=False,
    )
```

```python
import functools

import jax
import jax.numpy as jnp
from jax import lax
from jax.experimental import pallas as pl
from jax.experimental.pallas import tpu as pltpu
from jax.sharding import PartitionSpec as P

FR = 4
LAG = 1
CORES = 2
PIECES = 2
MIB = 1024 * 1024


def axis_split(devices):
    chips = devices // CORES
    x = 1
    while x * x * x * 8 <= chips and chips % (x * 2) == 0:
        x *= 2
    return chips // x, x


def scoped(devices, wide):
    return (24 if devices <= 32 else wide) * MIB


def split_rows(values):
    parts = []
    for _ in range(PIECES):
        part = values.astype(jnp.bfloat16)
        parts.append(part)
        values = values - part.astype(jnp.float32)
    return parts


def split_into(split_ref, blocks_ref, first):
    frames = split_ref.shape[0] // (3 * PIECES)
    atoms = split_ref.shape[1]
    group = min(frames, 32)

    def split_group(g, carry):
        blocks = blocks_ref[pl.ds(first + g * (group // FR), group // FR)]
        for c in range(3):
            values = blocks[:, c, :, :].reshape(group, atoms)
            for s, part in enumerate(split_rows(values)):
                row = (3 * s + c) * frames + g * group
                if frames != group:
                    row = pl.multiple_of(row, group)
                split_ref[pl.ds(row, group), :] = part
        return carry

    if frames == group:
        split_group(0, 0)
    else:
        lax.fori_loop(0, frames // group, split_group, 0)


def lengths(parts):
    rows = parts.shape[0] // PIECES
    frames = rows // 3
    difference = parts[:rows]
    for s in range(1, PIECES):
        difference = difference + parts[s * rows : (s + 1) * rows]
    squares = difference * difference
    return jnp.sqrt(squares[:frames] + squares[frames : 2 * frames] + squares[2 * frames :])


def distances(split, select):
    return lengths(jnp.dot(split, select, preferred_element_type=jnp.float32))


def ahead_of(rows):
    return jnp.concatenate([rows[LAG:], jnp.zeros((LAG, rows.shape[1]), rows.dtype)], axis=0)


def exchange_kernel(
    sizes,
    own_ref,
    pairs_hbm,
    counts_hbm,
    blocks_ref,
    select_ref,
    half_ref,
    weights_ref,
    pairs_ref,
    counts_ref,
    split_ref,
    load_sem,
    send_sem,
    recv_sem,
    share_sem,
    fetch_sem,
):
    zs, xs = sizes
    me = lax.axis_index("tm")
    core = lax.rem(me, CORES)
    x = lax.rem(me // CORES, xs)
    z = me // (CORES * xs)
    chunks, atoms, width = select_ref.shape
    frames = blocks_ref.shape[0] * FR

    def index(zi, xi, ci):
        return (zi * xs + xi) * CORES + ci

    def device(i):
        return {"tm": i}

    loads = [
        pltpu.make_async_copy(pairs_hbm, pairs_ref, load_sem.at[0]),
        pltpu.make_async_copy(own_ref, blocks_ref.at[me], load_sem.at[1]),
        pltpu.make_async_copy(counts_hbm, counts_ref, load_sem.at[2]),
    ]
    for load in loads:
        load.start()

    sibling = index(z, x, 1 - core)
    x_peers = [lax.rem(x + d, xs) for d in range(1, xs)]
    z_peers = [lax.rem(z + d, zs) for d in range(1, zs)]
    barrier = pltpu.get_barrier_semaphore()

    def greet(i):
        pl.semaphore_signal(
            barrier, inc=1, device_id=device(i), device_id_type=pl.DeviceIdType.MESH
        )

    for p in z_peers:
        greet(index(p, x, core))
    for p in x_peers:
        greet(index(z, p, core))
    greet(sibling)

    def build_select(j, carry):
        atom = lax.broadcasted_iota(jnp.int32, (atoms, width), 0).astype(jnp.int16)
        start = pl.multiple_of(j * width, width)
        first = pairs_ref[0:1, pl.ds(start, width)].astype(jnp.int16)
        second = pairs_ref[1:2, pl.ds(start, width)].astype(jnp.int16)
        one, zero = jnp.bfloat16(1.0), jnp.bfloat16(0.0)
        select_ref[j] = jnp.where(atom == first, one, jnp.where(atom == second, -one, zero))
        return carry

    marks = [chunks * p // 16 for p in BUILD]
    done = [0]

    def build_to(mark):
        if mark > done[0]:
            lax.fori_loop(done[0], mark, build_select, 0)
            done[0] = mark

    loads[0].wait()
    build_to(marks[0])
    pl.semaphore_wait(barrier, len(z_peers) + len(x_peers) + 1)

    sent = []

    def send(source, block, target, allowed):
        copy = pltpu.make_async_remote_copy(
            src_ref=source,
            dst_ref=blocks_ref.at[block],
            send_sem=send_sem.at[len(sent)],
            recv_sem=recv_sem.at[block],
            device_id=device(target),
            device_id_type=pl.DeviceIdType.MESH,
        )
        sent.append((copy, allowed))
        if allowed is None:
            copy.start()
        else:
            pl.when(allowed)(copy.start)

    def arrived(block):
        pltpu.make_async_remote_copy(
            src_ref=blocks_ref.at[block],
            dst_ref=blocks_ref.at[block],
            send_sem=send_sem.at[0],
            recv_sem=recv_sem.at[block],
            device_id=device(sibling),
            device_id_type=pl.DeviceIdType.MESH,
        ).wait_recv()

    for p in x_peers:
        send(own_ref, me, index(z, p, core), None)
    for d in range(1, zs):
        for sign in (1, -1):
            target = z + sign * d
            exists = target < zs if sign > 0 else target >= 0
            send(own_ref, me, index(target, x, core), exists)
    send(own_ref, me, sibling, None)

    def origins(d):
        for sign in (-1, 1) if d else (1,):
            origin = z + sign * d
            yield origin, None if d == 0 else (origin >= 0 if sign < 0 else origin < zs)

    def z_event(d):
        for origin, exists in origins(d):
            block = index(origin, x, core)
            pl.when(exists)(functools.partial(arrived, block))
            for p in x_peers:
                send(blocks_ref.at[block], block, index(z, p, core), exists)
            send(blocks_ref.at[block], block, sibling, exists)

    def x_event(d):
        for origin, exists in origins(d):
            for p in x_peers:
                block = index(origin, p, core)
                if exists is None:
                    arrived(block)
                else:
                    pl.when(exists)(functools.partial(arrived, block))
                send(blocks_ref.at[block], block, sibling, exists)

    near = zs // 2
    level = xs * CORES * FR
    half = z // near
    base = half * near

    build_to(marks[1])
    for loads_left in loads[1:]:
        loads_left.wait()
    frame = lax.broadcasted_iota(jnp.int32, (frames, 128), 0)

    def add_block(b, current):
        return jnp.where(frame // FR == b, counts_ref[b], current)

    current = lax.fori_loop(0, frames // FR, add_block, jnp.zeros((frames, 128), jnp.int32))
    valid = jnp.where(frame % FR < current, 1.0, 0.0)
    weights_ref[...] = valid * ahead_of(valid)
    per_core = chunks // CORES
    first_chunk = core * per_core

    def rows_of(r, owner):
        row = pl.multiple_of(lax.rem(z - base + r, near) * level, level)
        return half_ref.at[pl.ds(owner * per_core, per_core), pl.ds(row, level), :]

    def share(r, owner):
        return pltpu.make_async_remote_copy(
            src_ref=rows_of(r, owner),
            dst_ref=rows_of(r, owner),
            send_sem=share_sem.at[r],
            recv_sem=fetch_sem.at[r],
            device_id=device(sibling),
            device_id_type=pl.DeviceIdType.MESH,
        )

    def begin(r):
        zi = base + lax.rem(z - base + r, near)
        for xi in range(xs):
            arrived(index(zi, xi, 1 - core))
        split_into(split_ref, blocks_ref, zi * xs * CORES)

    def featurize(r, start, stop):
        row = pl.multiple_of(lax.rem(z - base + r, near) * level, level)

        def one(i, carry):
            j = first_chunk + i
            half_ref[j, pl.ds(row, level), :] = distances(split_ref[...], select_ref[j])
            return carry

        lax.fori_loop(per_core * start // 8, per_core * stop // 8, one, 0)
        if stop == 8:
            share(r, core).start()

    z_event(1)
    x_event(0)
    build_to(marks[2])
    begin(0)
    featurize(0, 0, OWN)
    z_event(2)
    build_to(chunks)
    featurize(0, OWN, 8)
    for d in range(1, near):
        if d > 1:
            z_event(d + 1)
        x_event(d)
    if near + 1 < zs:
        z_event(near + 1)
    for r in range(1, near):
        begin(r)
        featurize(r, 0, OTHER)
        if r == 1:
            x_event(near)
        featurize(r, OTHER, 8)
    for d in range(near + 1, zs):
        if d + 1 < zs:
            z_event(d + 1)
        x_event(d)

    for zi in range(near):
        for xi in range(xs):
            arrived(index((1 - half) * near + zi, xi, 1 - core))
    for r in range(near):
        share(r, core).wait_send()
        share(r, 1 - core).wait_recv()
    for copy, allowed in sent:
        if allowed is None:
            copy.wait_send()
        else:
            pl.when(allowed)(copy.wait_send)


BUILD = [2, 7, 16]
OWN = 3
OTHER = 4


def exchange(block, atom_pairs, frame_counts, devices, chunk):
    zs, xs = axis_split(devices)
    atoms = block.shape[2]
    frames = devices * FR
    chunks = atom_pairs.shape[1] // chunk
    dma = pltpu.SemaphoreType.DMA
    sends = (xs - 1) + 2 * (zs - 1) + 1 + 2 * (zs - 1) * xs + (2 * zs - 1) * (xs - 1)
    return pl.pallas_call(
        functools.partial(exchange_kernel, (zs, xs)),
        out_shape=(
            pltpu.VMEM((devices,) + block.shape, jnp.float32),
            pltpu.VMEM((chunks, atoms, chunk), jnp.bfloat16),
            pltpu.VMEM((chunks, frames // 2, chunk), jnp.float32),
            pltpu.VMEM((frames, 128), jnp.float32),
        ),
        in_specs=[pl.BlockSpec(memory_space=pltpu.HBM)] * 3,
        out_specs=(pl.BlockSpec(memory_space=pltpu.VMEM),) * 4,
        scratch_shapes=[
            pltpu.VMEM(atom_pairs.shape, jnp.int32),
            pltpu.SMEM(frame_counts.shape, jnp.int32),
            pltpu.VMEM((3 * PIECES * xs * CORES * FR, atoms), jnp.bfloat16),
            dma((3,)),
            dma((sends,)),
            dma((devices,)),
            dma((zs // 2,)),
            dma((zs // 2,)),
        ],
        compiler_params=pltpu.CompilerParams(
            collective_id=0, has_side_effects=True, vmem_limit_bytes=scoped(devices, 14)
        ),
        name="exchange",
    )(*(pltpu.with_memory_space_constraint(a, pltpu.HBM) for a in (block, atom_pairs, frame_counts)))


SLOTS = 4


def covariance_kernel(
    row_count,
    blocks_ref,
    select_ref,
    half_ref,
    weights_ref,
    mean_now_ref,
    mean_lag_ref,
    cov_now_ref,
    cov_lag_ref,
    left_ref,
    split_ref,
    parts_ref,
    early_ref,
    late_ref,
    tiles_ref,
    write_sem,
):
    chunks, part, width = half_ref.shape
    me = lax.axis_index("tm")
    held = blocks_ref.shape[0]
    mine = me // (held // 2)
    other = 1 - mine
    first = me * row_count // width

    def widened(rows):
        return jnp.concatenate([rows] * (width // 128), axis=1)

    scale = widened(1.0 / jnp.sum(weights_ref[...], axis=0, keepdims=True))

    def mean_of(rows):
        return jnp.sum(widened(weights_ref[...]) * rows, axis=0, keepdims=True) * scale

    def chunk_of(s):
        return lax.rem(first + s, chunks)

    def project(s):
        parts_ref[lax.rem(s, 2)] = jnp.dot(
            split_ref[...], select_ref[chunk_of(s)], preferred_element_type=jnp.float32
        )

    def center(s):
        j = chunk_of(s)
        slot = lax.rem(s, 2)
        ours = half_ref[j]
        theirs = lengths(parts_ref[slot])
        features = jnp.where(
            mine == 0,
            jnp.concatenate([ours, theirs], axis=0),
            jnp.concatenate([theirs, ours], axis=0),
        )
        ahead = ahead_of(features)
        mean_now = mean_of(features)
        mean_lag = mean_of(ahead)
        column = pl.ds(pl.multiple_of(j * width, width), width)
        mean_now_ref[:, column] = mean_now
        mean_lag_ref[:, column] = mean_lag
        early_ref[slot] = (features - mean_now).astype(jnp.bfloat16)
        late_ref[slot] = (ahead - mean_lag).astype(jnp.bfloat16)

    def writes(s):
        column = pl.multiple_of(chunk_of(s) * width, width)
        at = lax.rem(s, SLOTS)
        return [
            pltpu.make_async_copy(
                tiles_ref.at[at, o], ref.at[:, pl.ds(column, width)], write_sem.at[at, o]
            )
            for o, ref in enumerate((cov_now_ref, cov_lag_ref))
        ]

    def multiply(s):
        slot = lax.rem(s, 2)
        at = lax.rem(s, SLOTS)
        if row_count == width:
            left = left_ref[...]
        else:
            offset = lax.rem(me * row_count, width)
            left = left_ref[pl.ds(pl.multiple_of(offset, row_count), row_count), :]
        for o, ref in enumerate((early_ref, late_ref)):
            product = jnp.dot(left, ref[slot], preferred_element_type=jnp.float32)
            tiles_ref[at, o] = product * scale

    def finish(s):
        for write in writes(s):
            write.wait()

    split_into(split_ref, blocks_ref, other * (held // 2))
    project(0)
    project(1)
    center(0)
    left = early_ref[0].astype(jnp.float32) * widened(weights_ref[...])
    left_ref[...] = jnp.transpose(left).astype(jnp.bfloat16)

    def step(s, carry):
        pl.when(s >= SLOTS)(lambda: finish(s - SLOTS))
        multiply(s)
        center(s + 1)
        project(s + 2)
        for write in writes(s):
            write.start()
        return carry

    lax.fori_loop(0, chunks - 2, step, 0)
    for s in (chunks - 2, chunks - 1):
        finish(s - SLOTS)
        multiply(s)
        if s == chunks - 2:
            center(s + 1)
        for write in writes(s):
            write.start()
    for s in range(chunks - SLOTS, chunks):
        finish(s)


def covariances(blocks, select, half, weights, row_count):
    chunks, part, chunk = half.shape
    atoms = blocks.shape[3]
    width = chunks * chunk
    row = jax.ShapeDtypeStruct((1, width), jnp.float32)
    matrix = jax.ShapeDtypeStruct((row_count, width), jnp.float32)
    return pl.pallas_call(
        functools.partial(covariance_kernel, row_count),
        out_shape=(row, row, matrix, matrix),
        in_specs=[pl.BlockSpec(memory_space=pltpu.VMEM)] * 4,
        out_specs=(
            pl.BlockSpec(memory_space=pltpu.VMEM),
            pl.BlockSpec(memory_space=pltpu.VMEM),
            pl.BlockSpec(memory_space=pl.ANY),
            pl.BlockSpec(memory_space=pl.ANY),
        ),
        scratch_shapes=[
            pltpu.VMEM((chunk, 2 * part), jnp.bfloat16),
            pltpu.VMEM((3 * PIECES * part, atoms), jnp.bfloat16),
            pltpu.VMEM((2, 3 * PIECES * part, chunk), jnp.float32),
            pltpu.VMEM((2, 2 * part, chunk), jnp.bfloat16),
            pltpu.VMEM((2, 2 * part, chunk), jnp.bfloat16),
            pltpu.VMEM((SLOTS, 2, row_count, chunk), jnp.float32),
            pltpu.SemaphoreType.DMA((SLOTS, 2)),
        ],
        compiler_params=pltpu.CompilerParams(
            vmem_limit_bytes=scoped(blocks.shape[0], 56)
        ),
        name="covariances",
    )(blocks, select, half, weights)


def body(positions, atom_pairs, frame_counts):
    devices = lax.axis_size("tm")
    width = atom_pairs.shape[1]
    row_count = width // devices
    chunk = 512 if devices <= 32 else 128
    gathered = exchange(
        jnp.transpose(positions, (1, 0, 2)), atom_pairs, frame_counts, devices, chunk
    )
    mean_now, mean_lag, cov_now, cov_lag = covariances(*gathered, row_count)
    return (mean_now.reshape(width), mean_lag.reshape(width), cov_now, cov_lag)


def solution(mesh):
    return jax.shard_map(
        body,
        mesh=mesh,
        in_specs=(P(("groups", "tm"), None, None), P(), P("groups")),
        out_specs=(P("groups"), P("groups"), P(("groups", "tm"), None), P(("groups", "tm"), None)),
        check_vma=False,
    )
```

```python
import functools

import jax
import jax.numpy as jnp
from jax import lax
from jax.experimental import pallas as pl
from jax.experimental.pallas import tpu as pltpu
from jax.sharding import PartitionSpec as P

FR = 4
LAG = 1
CORES = 2
PIECES = 2
MIB = 1024 * 1024


def axis_split(devices):
    chips = devices // CORES
    x = 1
    while x * x * x * 8 <= chips and chips % (x * 2) == 0:
        x *= 2
    return chips // x, x


def scoped(devices, wide):
    return (24 if devices <= 32 else wide) * MIB


def split_rows(values):
    parts = []
    for _ in range(PIECES):
        part = values.astype(jnp.bfloat16)
        parts.append(part)
        values = values - part.astype(jnp.float32)
    return parts


def split_into(split_ref, blocks_ref, first):
    frames = split_ref.shape[0] // (3 * PIECES)
    atoms = split_ref.shape[1]
    group = min(frames, 32)

    def split_group(g, carry):
        blocks = blocks_ref[pl.ds(first + g * (group // FR), group // FR)]
        for c in range(3):
            values = blocks[:, c, :, :].reshape(group, atoms)
            for s, part in enumerate(split_rows(values)):
                row = (3 * s + c) * frames + g * group
                if frames != group:
                    row = pl.multiple_of(row, group)
                split_ref[pl.ds(row, group), :] = part
        return carry

    if frames == group:
        split_group(0, 0)
    else:
        lax.fori_loop(0, frames // group, split_group, 0)


def lengths(parts):
    rows = parts.shape[0] // PIECES
    frames = rows // 3
    difference = parts[:rows]
    for s in range(1, PIECES):
        difference = difference + parts[s * rows : (s + 1) * rows]
    squares = difference * difference
    return jnp.sqrt(squares[:frames] + squares[frames : 2 * frames] + squares[2 * frames :])


def distances(split, select):
    return lengths(jnp.dot(split, select, preferred_element_type=jnp.float32))


def ahead_of(rows):
    return jnp.concatenate([rows[LAG:], jnp.zeros((LAG, rows.shape[1]), rows.dtype)], axis=0)


def exchange_kernel(
    sizes,
    own_ref,
    pairs_hbm,
    counts_hbm,
    blocks_ref,
    select_ref,
    half_ref,
    weights_ref,
    pairs_ref,
    counts_ref,
    split_ref,
    load_sem,
    send_sem,
    recv_sem,
    share_sem,
    fetch_sem,
):
    zs, xs = sizes
    me = lax.axis_index("tm")
    core = lax.rem(me, CORES)
    x = lax.rem(me // CORES, xs)
    z = me // (CORES * xs)
    chunks, atoms, width = select_ref.shape
    frames = blocks_ref.shape[0] * FR

    def index(zi, xi, ci):
        return (zi * xs + xi) * CORES + ci

    def device(i):
        return {"tm": i}

    loads = [
        pltpu.make_async_copy(pairs_hbm, pairs_ref, load_sem.at[0]),
        pltpu.make_async_copy(own_ref, blocks_ref.at[me], load_sem.at[1]),
        pltpu.make_async_copy(counts_hbm, counts_ref, load_sem.at[2]),
    ]
    for load in loads:
        load.start()

    sibling = index(z, x, 1 - core)
    x_peers = [lax.rem(x + d, xs) for d in range(1, xs)]
    z_peers = [lax.rem(z + d, zs) for d in range(1, zs)]
    barrier = pltpu.get_barrier_semaphore()

    def greet(i):
        pl.semaphore_signal(
            barrier, inc=1, device_id=device(i), device_id_type=pl.DeviceIdType.MESH
        )

    for p in z_peers:
        greet(index(p, x, core))
    for p in x_peers:
        greet(index(z, p, core))
    greet(sibling)

    def build_select(j, carry):
        atom = lax.broadcasted_iota(jnp.int32, (atoms, width), 0).astype(jnp.int16)
        start = pl.multiple_of(j * width, width)
        first = pairs_ref[0:1, pl.ds(start, width)].astype(jnp.int16)
        second = pairs_ref[1:2, pl.ds(start, width)].astype(jnp.int16)
        one, zero = jnp.bfloat16(1.0), jnp.bfloat16(0.0)
        select_ref[j] = jnp.where(atom == first, one, jnp.where(atom == second, -one, zero))
        return carry

    marks = [chunks * p // 16 for p in BUILD]
    done = [0]

    def build_to(mark):
        if mark > done[0]:
            lax.fori_loop(done[0], mark, build_select, 0)
            done[0] = mark

    loads[0].wait()
    build_to(marks[0])
    pl.semaphore_wait(barrier, len(z_peers) + len(x_peers) + 1)

    sent = []

    def send(source, block, target, allowed):
        copy = pltpu.make_async_remote_copy(
            src_ref=source,
            dst_ref=blocks_ref.at[block],
            send_sem=send_sem.at[len(sent)],
            recv_sem=recv_sem.at[block],
            device_id=device(target),
            device_id_type=pl.DeviceIdType.MESH,
        )
        sent.append((copy, allowed))
        if allowed is None:
            copy.start()
        else:
            pl.when(allowed)(copy.start)

    def arrived(block):
        pltpu.make_async_remote_copy(
            src_ref=blocks_ref.at[block],
            dst_ref=blocks_ref.at[block],
            send_sem=send_sem.at[0],
            recv_sem=recv_sem.at[block],
            device_id=device(sibling),
            device_id_type=pl.DeviceIdType.MESH,
        ).wait_recv()

    send(own_ref, me, sibling, None)
    for p in x_peers:
        send(own_ref, me, index(z, p, core), None)
    for d in range(1, zs):
        for sign in (1, -1) if d != 2 else ():
            target = z + sign * d
            exists = target < zs if sign > 0 else target >= 0
            send(own_ref, me, index(target, x, core), exists)

    def origins(d):
        for sign in (-1, 1) if d else (1,):
            origin = z + sign * d
            yield origin, None if d == 0 else (origin >= 0 if sign < 0 else origin < zs)

    def z_event(d):
        for origin, exists in origins(d):
            block = index(origin, x, core)
            pl.when(exists)(functools.partial(arrived, block))
            if d == 1:
                onward = 2 * z - origin
                inside = jnp.logical_and(onward >= 0, onward < zs)
                passed = jnp.logical_and(exists, inside)
                send(blocks_ref.at[block], block, index(onward, x, core), passed)
            send(blocks_ref.at[block], block, sibling, exists)
            for p in x_peers:
                send(blocks_ref.at[block], block, index(z, p, core), exists)

    def x_event(d):
        for origin, exists in origins(d):
            for p in x_peers:
                block = index(origin, p, core)
                if exists is None:
                    arrived(block)
                else:
                    pl.when(exists)(functools.partial(arrived, block))
                send(blocks_ref.at[block], block, sibling, exists)

    near = zs // 2
    level = xs * CORES * FR
    half = z // near
    base = half * near

    build_to(marks[1])
    for loads_left in loads[1:]:
        loads_left.wait()
    frame = lax.broadcasted_iota(jnp.int32, (frames, 128), 0)

    def add_block(b, current):
        return jnp.where(frame // FR == b, counts_ref[b], current)

    current = lax.fori_loop(0, frames // FR, add_block, jnp.zeros((frames, 128), jnp.int32))
    valid = jnp.where(frame % FR < current, 1.0, 0.0)
    weights_ref[...] = valid * ahead_of(valid)
    per_core = chunks // CORES
    first_chunk = core * per_core

    def rows_of(r, p, owner):
        row = pl.multiple_of(lax.rem(z - base + r, near) * level, level)
        part = per_core // 2
        start = owner * per_core + p * part
        return half_ref.at[pl.ds(start, part), pl.ds(row, level), :]

    def share(r, p, owner):
        return pltpu.make_async_remote_copy(
            src_ref=rows_of(r, p, owner),
            dst_ref=rows_of(r, p, owner),
            send_sem=share_sem.at[r, p],
            recv_sem=fetch_sem.at[r, p],
            device_id=device(sibling),
            device_id_type=pl.DeviceIdType.MESH,
        )

    def begin(r):
        zi = base + lax.rem(z - base + r, near)
        for xi in range(xs):
            arrived(index(zi, xi, 1 - core))
        split_into(split_ref, blocks_ref, zi * xs * CORES)

    def featurize(r, start, stop):
        row = pl.multiple_of(lax.rem(z - base + r, near) * level, level)

        def one(i, carry):
            j = first_chunk + i
            half_ref[j, pl.ds(row, level), :] = distances(split_ref[...], select_ref[j])
            return carry

        lax.fori_loop(per_core * start // 8, per_core * stop // 8, one, 0)
        if start < 4 <= stop:
            share(r, 0, core).start()
        if stop == 8:
            share(r, 1, core).start()

    drained = [0]

    def drain(upto):
        for copy, allowed in sent[drained[0] : upto]:
            if allowed is None:
                copy.wait_send()
            else:
                pl.when(allowed)(copy.wait_send)
        drained[0] = upto

    z_event(1)
    x_event(0)
    first_sends = len(sent)
    build_to(chunks)
    begin(0)
    featurize(0, 0, OWN)
    for d in reversed(range(2, zs)):
        z_event(d)
    for d in range(1, near):
        x_event(d)
    featurize(0, OWN, 8)
    for r in range(1, near):
        begin(r)
        featurize(r, 0, OTHER)
        if r == near - 1:
            drain(first_sends)
            for d in range(near, zs):
                x_event(d)
        featurize(r, OTHER, 8)

    for zi in range(near):
        for xi in range(xs):
            arrived(index((1 - half) * near + zi, xi, 1 - core))
    for r in range(near):
        for p in (0, 1):
            share(r, p, core).wait_send()
            share(r, p, 1 - core).wait_recv()
    drain(len(sent))


BUILD = [2, 9, 16]
OWN = 4
OTHER = 4


def exchange(block, atom_pairs, frame_counts, devices, chunk):
    zs, xs = axis_split(devices)
    atoms = block.shape[2]
    frames = devices * FR
    chunks = atom_pairs.shape[1] // chunk
    dma = pltpu.SemaphoreType.DMA
    sends = 2 + (xs - 1) + 2 * (zs - 1) + 1 + 2 * (zs - 1) * xs + (2 * zs - 1) * (xs - 1)
    return pl.pallas_call(
        functools.partial(exchange_kernel, (zs, xs)),
        out_shape=(
            pltpu.VMEM((devices,) + block.shape, jnp.float32),
            pltpu.VMEM((chunks, atoms, chunk), jnp.bfloat16),
            pltpu.VMEM((chunks, frames // 2, chunk), jnp.float32),
            pltpu.VMEM((frames, 128), jnp.float32),
        ),
        in_specs=[pl.BlockSpec(memory_space=pltpu.HBM)] * 3,
        out_specs=(pl.BlockSpec(memory_space=pltpu.VMEM),) * 4,
        scratch_shapes=[
            pltpu.VMEM(atom_pairs.shape, jnp.int32),
            pltpu.SMEM(frame_counts.shape, jnp.int32),
            pltpu.VMEM((3 * PIECES * xs * CORES * FR, atoms), jnp.bfloat16),
            dma((3,)),
            dma((sends,)),
            dma((devices,)),
            dma((zs // 2, 2)),
            dma((zs // 2, 2)),
        ],
        compiler_params=pltpu.CompilerParams(
            collective_id=0, has_side_effects=True, vmem_limit_bytes=scoped(devices, 14)
        ),
        name="exchange",
    )(*(pltpu.with_memory_space_constraint(a, pltpu.HBM) for a in (block, atom_pairs, frame_counts)))


SLOTS = 4


def covariance_kernel(
    row_count,
    blocks_ref,
    select_ref,
    half_ref,
    weights_ref,
    mean_now_ref,
    mean_lag_ref,
    cov_now_ref,
    cov_lag_ref,
    left_ref,
    split_ref,
    parts_ref,
    early_ref,
    late_ref,
    tiles_ref,
    write_sem,
):
    chunks, part, width = half_ref.shape
    me = lax.axis_index("tm")
    held = blocks_ref.shape[0]
    mine = me // (held // 2)
    other = 1 - mine
    first = me * row_count // width

    def widened(rows):
        return jnp.concatenate([rows] * (width // 128), axis=1)

    scale = widened(1.0 / jnp.sum(weights_ref[...], axis=0, keepdims=True))

    def mean_of(rows):
        return jnp.sum(widened(weights_ref[...]) * rows, axis=0, keepdims=True) * scale

    def chunk_of(s):
        return lax.rem(first + s, chunks)

    def project(s):
        parts_ref[lax.rem(s, 2)] = jnp.dot(
            split_ref[...], select_ref[chunk_of(s)], preferred_element_type=jnp.float32
        )

    def center(s):
        j = chunk_of(s)
        slot = lax.rem(s, 2)
        ours = half_ref[j]
        theirs = lengths(parts_ref[slot])
        features = jnp.where(
            mine == 0,
            jnp.concatenate([ours, theirs], axis=0),
            jnp.concatenate([theirs, ours], axis=0),
        )
        ahead = ahead_of(features)
        mean_now = mean_of(features)
        mean_lag = mean_of(ahead)
        column = pl.ds(pl.multiple_of(j * width, width), width)
        mean_now_ref[:, column] = mean_now
        mean_lag_ref[:, column] = mean_lag
        early_ref[slot] = (features - mean_now).astype(jnp.bfloat16)
        late_ref[slot] = (ahead - mean_lag).astype(jnp.bfloat16)

    def writes(s):
        column = pl.multiple_of(chunk_of(s) * width, width)
        at = lax.rem(s, SLOTS)
        return [
            pltpu.make_async_copy(
                tiles_ref.at[at, o], ref.at[:, pl.ds(column, width)], write_sem.at[at, o]
            )
            for o, ref in enumerate((cov_now_ref, cov_lag_ref))
        ]

    def multiply(s):
        slot = lax.rem(s, 2)
        at = lax.rem(s, SLOTS)
        if row_count == width:
            left = left_ref[...]
        else:
            offset = lax.rem(me * row_count, width)
            left = left_ref[pl.ds(pl.multiple_of(offset, row_count), row_count), :]
        for o, ref in enumerate((early_ref, late_ref)):
            product = jnp.dot(left, ref[slot], preferred_element_type=jnp.float32)
            tiles_ref[at, o] = product * scale

    def finish(s):
        for write in writes(s):
            write.wait()

    split_into(split_ref, blocks_ref, other * (held // 2))
    project(0)
    project(1)
    center(0)
    left = early_ref[0].astype(jnp.float32) * widened(weights_ref[...])
    left_ref[...] = jnp.transpose(left).astype(jnp.bfloat16)

    def step(s, carry):
        pl.when(s >= SLOTS)(lambda: finish(s - SLOTS))
        multiply(s)
        center(s + 1)
        project(s + 2)
        for write in writes(s):
            write.start()
        return carry

    lax.fori_loop(0, chunks - 2, step, 0)
    for s in (chunks - 2, chunks - 1):
        finish(s - SLOTS)
        multiply(s)
        if s == chunks - 2:
            center(s + 1)
        for write in writes(s):
            write.start()
    for s in range(chunks - SLOTS, chunks):
        finish(s)


def covariances(blocks, select, half, weights, row_count):
    chunks, part, chunk = half.shape
    atoms = blocks.shape[3]
    width = chunks * chunk
    row = jax.ShapeDtypeStruct((1, width), jnp.float32)
    matrix = jax.ShapeDtypeStruct((row_count, width), jnp.float32)
    return pl.pallas_call(
        functools.partial(covariance_kernel, row_count),
        out_shape=(row, row, matrix, matrix),
        in_specs=[pl.BlockSpec(memory_space=pltpu.VMEM)] * 4,
        out_specs=(
            pl.BlockSpec(memory_space=pltpu.VMEM),
            pl.BlockSpec(memory_space=pltpu.VMEM),
            pl.BlockSpec(memory_space=pl.ANY),
            pl.BlockSpec(memory_space=pl.ANY),
        ),
        scratch_shapes=[
            pltpu.VMEM((chunk, 2 * part), jnp.bfloat16),
            pltpu.VMEM((3 * PIECES * part, atoms), jnp.bfloat16),
            pltpu.VMEM((2, 3 * PIECES * part, chunk), jnp.float32),
            pltpu.VMEM((2, 2 * part, chunk), jnp.bfloat16),
            pltpu.VMEM((2, 2 * part, chunk), jnp.bfloat16),
            pltpu.VMEM((SLOTS, 2, row_count, chunk), jnp.float32),
            pltpu.SemaphoreType.DMA((SLOTS, 2)),
        ],
        compiler_params=pltpu.CompilerParams(
            vmem_limit_bytes=scoped(blocks.shape[0], 56)
        ),
        name="covariances",
    )(blocks, select, half, weights)


def body(positions, atom_pairs, frame_counts):
    devices = lax.axis_size("tm")
    width = atom_pairs.shape[1]
    row_count = width // devices
    chunk = 512 if devices <= 32 else 128
    gathered = exchange(
        jnp.transpose(positions, (1, 0, 2)), atom_pairs, frame_counts, devices, chunk
    )
    mean_now, mean_lag, cov_now, cov_lag = covariances(*gathered, row_count)
    return (mean_now.reshape(width), mean_lag.reshape(width), cov_now, cov_lag)


def solution(mesh):
    return jax.shard_map(
        body,
        mesh=mesh,
        in_specs=(P(("groups", "tm"), None, None), P(), P("groups")),
        out_specs=(P("groups"), P("groups"), P(("groups", "tm"), None), P(("groups", "tm"), None)),
        check_vma=False,
    )
```

```python
import functools

import jax
import jax.numpy as jnp
from jax import lax
from jax.experimental import pallas as pl
from jax.experimental.pallas import tpu as pltpu
from jax.sharding import PartitionSpec as P

FR = 4
LAG = 1
CORES = 2
PIECES = 2
MIB = 1024 * 1024


def axis_split(devices):
    chips = devices // CORES
    x = 1
    while x * x * x * 8 <= chips and chips % (x * 2) == 0:
        x *= 2
    return chips // x, x


def scoped(devices, wide):
    return (24 if devices <= 32 else wide) * MIB


def split_rows(values):
    parts = []
    for _ in range(PIECES):
        part = values.astype(jnp.bfloat16)
        parts.append(part)
        values = values - part.astype(jnp.float32)
    return parts


def split_into(split_ref, blocks_ref, first):
    frames = split_ref.shape[0] // (3 * PIECES)
    atoms = split_ref.shape[1]
    group = min(frames, 32)

    def split_group(g, carry):
        blocks = blocks_ref[pl.ds(first + g * (group // FR), group // FR)]
        for c in range(3):
            values = blocks[:, c, :, :].reshape(group, atoms)
            for s, part in enumerate(split_rows(values)):
                row = (3 * s + c) * frames + g * group
                if frames != group:
                    row = pl.multiple_of(row, group)
                split_ref[pl.ds(row, group), :] = part
        return carry

    if frames == group:
        split_group(0, 0)
    else:
        lax.fori_loop(0, frames // group, split_group, 0)


def lengths(parts):
    rows = parts.shape[0] // PIECES
    frames = rows // 3
    difference = parts[:rows]
    for s in range(1, PIECES):
        difference = difference + parts[s * rows : (s + 1) * rows]
    squares = difference * difference
    return jnp.sqrt(squares[:frames] + squares[frames : 2 * frames] + squares[2 * frames :])


def distances(split, select):
    return lengths(jnp.dot(split, select, preferred_element_type=jnp.float32))


def ahead_of(rows):
    return jnp.concatenate([rows[LAG:], jnp.zeros((LAG, rows.shape[1]), rows.dtype)], axis=0)


def exchange_kernel(
    sizes,
    own_ref,
    pairs_hbm,
    counts_hbm,
    blocks_ref,
    select_ref,
    half_ref,
    weights_ref,
    pairs_ref,
    counts_ref,
    split_ref,
    load_sem,
    send_sem,
    recv_sem,
    share_sem,
    fetch_sem,
):
    zs, xs = sizes
    me = lax.axis_index("tm")
    core = lax.rem(me, CORES)
    x = lax.rem(me // CORES, xs)
    z = me // (CORES * xs)
    chunks, atoms, width = select_ref.shape
    frames = blocks_ref.shape[0] * FR

    def index(zi, xi, ci):
        return (zi * xs + xi) * CORES + ci

    def device(i):
        return {"tm": i}

    loads = [
        pltpu.make_async_copy(pairs_hbm, pairs_ref, load_sem.at[0]),
        pltpu.make_async_copy(own_ref, blocks_ref.at[me], load_sem.at[1]),
        pltpu.make_async_copy(counts_hbm, counts_ref, load_sem.at[2]),
    ]
    for load in loads:
        load.start()

    sibling = index(z, x, 1 - core)
    x_peers = [lax.rem(x + d, xs) for d in range(1, xs)]
    z_peers = [lax.rem(z + d, zs) for d in range(1, zs)]
    barrier = pltpu.get_barrier_semaphore()

    def greet(i):
        pl.semaphore_signal(
            barrier, inc=1, device_id=device(i), device_id_type=pl.DeviceIdType.MESH
        )

    for p in z_peers:
        greet(index(p, x, core))
    for p in x_peers:
        greet(index(z, p, core))
    greet(sibling)

    def build_select(j, carry):
        atom = lax.broadcasted_iota(jnp.int32, (atoms, width), 0).astype(jnp.int16)
        start = pl.multiple_of(j * width, width)
        first = pairs_ref[0:1, pl.ds(start, width)].astype(jnp.int16)
        second = pairs_ref[1:2, pl.ds(start, width)].astype(jnp.int16)
        one, zero = jnp.bfloat16(1.0), jnp.bfloat16(0.0)
        select_ref[j] = jnp.where(atom == first, one, jnp.where(atom == second, -one, zero))
        return carry

    marks = [chunks * p // 16 for p in BUILD]
    done = [0]

    def build_to(mark):
        if mark > done[0]:
            lax.fori_loop(done[0], mark, build_select, 0)
            done[0] = mark

    loads[0].wait()
    build_to(marks[0])
    pl.semaphore_wait(barrier, len(z_peers) + len(x_peers) + 1)

    sent = []

    def send(source, block, target, allowed):
        copy = pltpu.make_async_remote_copy(
            src_ref=source,
            dst_ref=blocks_ref.at[block],
            send_sem=send_sem.at[len(sent)],
            recv_sem=recv_sem.at[block],
            device_id=device(target),
            device_id_type=pl.DeviceIdType.MESH,
        )
        sent.append((copy, allowed))
        if allowed is None:
            copy.start()
        else:
            pl.when(allowed)(copy.start)

    def arrived(block):
        pltpu.make_async_remote_copy(
            src_ref=blocks_ref.at[block],
            dst_ref=blocks_ref.at[block],
            send_sem=send_sem.at[0],
            recv_sem=recv_sem.at[block],
            device_id=device(sibling),
            device_id_type=pl.DeviceIdType.MESH,
        ).wait_recv()

    send(own_ref, me, sibling, None)
    for p in x_peers:
        send(own_ref, me, index(z, p, core), None)
    for d in range(1, zs):
        for sign in (1, -1) if d != 2 else ():
            target = z + sign * d
            exists = target < zs if sign > 0 else target >= 0
            send(own_ref, me, index(target, x, core), exists)

    def origins(d):
        for sign in (-1, 1) if d else (1,):
            origin = z + sign * d
            yield origin, None if d == 0 else (origin >= 0 if sign < 0 else origin < zs)

    def z_event(d):
        for origin, exists in origins(d):
            block = index(origin, x, core)
            pl.when(exists)(functools.partial(arrived, block))
            if d == 1:
                onward = 2 * z - origin
                inside = jnp.logical_and(onward >= 0, onward < zs)
                passed = jnp.logical_and(exists, inside)
                send(blocks_ref.at[block], block, index(onward, x, core), passed)
            send(blocks_ref.at[block], block, sibling, exists)
            for p in x_peers:
                send(blocks_ref.at[block], block, index(z, p, core), exists)

    def x_event(d):
        for origin, exists in origins(d):
            for p in x_peers:
                block = index(origin, p, core)
                if exists is None:
                    arrived(block)
                else:
                    pl.when(exists)(functools.partial(arrived, block))
                send(blocks_ref.at[block], block, sibling, exists)

    near = zs // 2
    level = xs * CORES * FR
    half = z // near
    base = half * near

    build_to(marks[1])
    for loads_left in loads[1:]:
        loads_left.wait()
    frame = lax.broadcasted_iota(jnp.int32, (frames, 128), 0)

    def add_block(b, current):
        return jnp.where(frame // FR == b, counts_ref[b], current)

    current = lax.fori_loop(0, frames // FR, add_block, jnp.zeros((frames, 128), jnp.int32))
    valid = jnp.where(frame % FR < current, 1.0, 0.0)
    weights_ref[...] = valid * ahead_of(valid)
    per_core = chunks // CORES
    first_chunk = core * per_core

    def rows_of(r, p, owner):
        row = pl.multiple_of(lax.rem(z - base + r, near) * level, level)
        part = per_core // 2
        start = owner * per_core + p * part
        return half_ref.at[pl.ds(start, part), pl.ds(row, level), :]

    def share(r, p, owner):
        return pltpu.make_async_remote_copy(
            src_ref=rows_of(r, p, owner),
            dst_ref=rows_of(r, p, owner),
            send_sem=share_sem.at[r, p],
            recv_sem=fetch_sem.at[r, p],
            device_id=device(sibling),
            device_id_type=pl.DeviceIdType.MESH,
        )

    def begin(r):
        zi = base + lax.rem(z - base + r, near)
        for xi in range(xs):
            arrived(index(zi, xi, 1 - core))
        split_into(split_ref, blocks_ref, zi * xs * CORES)

    def featurize(r, start, stop):
        row = pl.multiple_of(lax.rem(z - base + r, near) * level, level)

        def one(i, carry):
            j = first_chunk + i
            half_ref[j, pl.ds(row, level), :] = distances(split_ref[...], select_ref[j])
            return carry

        lax.fori_loop(per_core * start // 8, per_core * stop // 8, one, 0)
        if start < 4 <= stop:
            share(r, 0, core).start()
        if stop == 8:
            share(r, 1, core).start()

    drained = [0]

    def drain(upto):
        for copy, allowed in sent[drained[0] : upto]:
            if allowed is None:
                copy.wait_send()
            else:
                pl.when(allowed)(copy.wait_send)
        drained[0] = upto

    z_event(1)
    x_event(0)
    first_sends = len(sent)
    build_to(chunks)
    begin(0)
    featurize(0, 0, OWN)
    for d in reversed(range(2, zs)):
        z_event(d)
    for d in range(1, near):
        x_event(d)
    featurize(0, OWN, 8)
    for r in range(1, near):
        begin(r)
        featurize(r, 0, OTHER)
        if r == near - 1:
            drain(first_sends)
            for d in range(near, zs):
                x_event(d)
        featurize(r, OTHER, 8)

    for zi in range(near):
        for xi in range(xs):
            arrived(index((1 - half) * near + zi, xi, 1 - core))
    for r in range(near):
        for p in (0, 1):
            share(r, p, core).wait_send()
            share(r, p, 1 - core).wait_recv()
    drain(len(sent))


BUILD = [2, 12, 16]
OWN = 4
OTHER = 7


def exchange(block, atom_pairs, frame_counts, devices, chunk):
    zs, xs = axis_split(devices)
    atoms = block.shape[2]
    frames = devices * FR
    chunks = atom_pairs.shape[1] // chunk
    dma = pltpu.SemaphoreType.DMA
    sends = 2 + (xs - 1) + 2 * (zs - 1) + 1 + 2 * (zs - 1) * xs + (2 * zs - 1) * (xs - 1)
    return pl.pallas_call(
        functools.partial(exchange_kernel, (zs, xs)),
        out_shape=(
            pltpu.VMEM((devices,) + block.shape, jnp.float32),
            pltpu.VMEM((chunks, atoms, chunk), jnp.bfloat16),
            pltpu.VMEM((chunks, frames // 2, chunk), jnp.float32),
            pltpu.VMEM((frames, 128), jnp.float32),
        ),
        in_specs=[pl.BlockSpec(memory_space=pltpu.HBM)] * 3,
        out_specs=(pl.BlockSpec(memory_space=pltpu.VMEM),) * 4,
        scratch_shapes=[
            pltpu.VMEM(atom_pairs.shape, jnp.int32),
            pltpu.SMEM(frame_counts.shape, jnp.int32),
            pltpu.VMEM((3 * PIECES * xs * CORES * FR, atoms), jnp.bfloat16),
            dma((3,)),
            dma((sends,)),
            dma((devices,)),
            dma((zs // 2, 2)),
            dma((zs // 2, 2)),
        ],
        compiler_params=pltpu.CompilerParams(
            collective_id=0, has_side_effects=True, vmem_limit_bytes=scoped(devices, 14)
        ),
        name="exchange",
    )(*(pltpu.with_memory_space_constraint(a, pltpu.HBM) for a in (block, atom_pairs, frame_counts)))


SLOTS = 4


def covariance_kernel(
    row_count,
    blocks_ref,
    select_ref,
    half_ref,
    weights_ref,
    mean_now_ref,
    mean_lag_ref,
    cov_now_ref,
    cov_lag_ref,
    left_ref,
    split_ref,
    parts_ref,
    early_ref,
    late_ref,
    tiles_ref,
    write_sem,
):
    chunks, part, width = half_ref.shape
    me = lax.axis_index("tm")
    held = blocks_ref.shape[0]
    mine = me // (held // 2)
    other = 1 - mine
    first = me * row_count // width

    def widened(rows):
        return jnp.concatenate([rows] * (width // 128), axis=1)

    scale = widened(1.0 / jnp.sum(weights_ref[...], axis=0, keepdims=True))

    def mean_of(rows):
        return jnp.sum(widened(weights_ref[...]) * rows, axis=0, keepdims=True) * scale

    def chunk_of(s):
        return lax.rem(first + s, chunks)

    def project(s):
        parts_ref[lax.rem(s, 2)] = jnp.dot(
            split_ref[...], select_ref[chunk_of(s)], preferred_element_type=jnp.float32
        )

    def center(s):
        j = chunk_of(s)
        slot = lax.rem(s, 2)
        ours = half_ref[j]
        theirs = lengths(parts_ref[slot])
        features = jnp.where(
            mine == 0,
            jnp.concatenate([ours, theirs], axis=0),
            jnp.concatenate([theirs, ours], axis=0),
        )
        ahead = ahead_of(features)
        mean_now = mean_of(features)
        mean_lag = mean_of(ahead)
        column = pl.ds(pl.multiple_of(j * width, width), width)
        mean_now_ref[:, column] = mean_now
        mean_lag_ref[:, column] = mean_lag
        early_ref[slot] = (features - mean_now).astype(jnp.bfloat16)
        late_ref[slot] = (ahead - mean_lag).astype(jnp.bfloat16)

    def writes(s):
        column = pl.multiple_of(chunk_of(s) * width, width)
        at = lax.rem(s, SLOTS)
        return [
            pltpu.make_async_copy(
                tiles_ref.at[at, o], ref.at[:, pl.ds(column, width)], write_sem.at[at, o]
            )
            for o, ref in enumerate((cov_now_ref, cov_lag_ref))
        ]

    def multiply(s):
        slot = lax.rem(s, 2)
        at = lax.rem(s, SLOTS)
        if row_count == width:
            left = left_ref[...]
        else:
            offset = lax.rem(me * row_count, width)
            left = left_ref[pl.ds(pl.multiple_of(offset, row_count), row_count), :]
        n = max(row_count // 4, 16)
        for r in range(0, row_count, n):
            for o, ref in enumerate((early_ref, late_ref)):
                product = jnp.dot(left[r : r + n], ref[slot], preferred_element_type=jnp.float32)
                tiles_ref[at, o, r : r + n] = product * scale

    def finish(s):
        for write in writes(s):
            write.wait()

    split_into(split_ref, blocks_ref, other * (held // 2))
    project(0)
    project(1)
    center(0)
    left = early_ref[0].astype(jnp.float32) * widened(weights_ref[...])
    left_ref[...] = jnp.transpose(left).astype(jnp.bfloat16)

    def step(s, carry):
        pl.when(s >= SLOTS)(lambda: finish(s - SLOTS))
        multiply(s)
        center(s + 1)
        project(s + 2)
        for write in writes(s):
            write.start()
        return carry

    lax.fori_loop(0, chunks - 2, step, 0)
    for s in (chunks - 2, chunks - 1):
        finish(s - SLOTS)
        multiply(s)
        if s == chunks - 2:
            center(s + 1)
        for write in writes(s):
            write.start()
    for s in range(chunks - SLOTS, chunks):
        finish(s)


def covariances(blocks, select, half, weights, row_count):
    chunks, part, chunk = half.shape
    atoms = blocks.shape[3]
    width = chunks * chunk
    row = jax.ShapeDtypeStruct((1, width), jnp.float32)
    matrix = jax.ShapeDtypeStruct((row_count, width), jnp.float32)
    return pl.pallas_call(
        functools.partial(covariance_kernel, row_count),
        out_shape=(row, row, matrix, matrix),
        in_specs=[pl.BlockSpec(memory_space=pltpu.VMEM)] * 4,
        out_specs=(
            pl.BlockSpec(memory_space=pltpu.VMEM),
            pl.BlockSpec(memory_space=pltpu.VMEM),
            pl.BlockSpec(memory_space=pl.ANY),
            pl.BlockSpec(memory_space=pl.ANY),
        ),
        scratch_shapes=[
            pltpu.VMEM((chunk, 2 * part), jnp.bfloat16),
            pltpu.VMEM((3 * PIECES * part, atoms), jnp.bfloat16),
            pltpu.VMEM((2, 3 * PIECES * part, chunk), jnp.float32),
            pltpu.VMEM((2, 2 * part, chunk), jnp.bfloat16),
            pltpu.VMEM((2, 2 * part, chunk), jnp.bfloat16),
            pltpu.VMEM((SLOTS, 2, row_count, chunk), jnp.float32),
            pltpu.SemaphoreType.DMA((SLOTS, 2)),
        ],
        compiler_params=pltpu.CompilerParams(
            vmem_limit_bytes=scoped(blocks.shape[0], 56)
        ),
        name="covariances",
    )(blocks, select, half, weights)


def body(positions, atom_pairs, frame_counts):
    devices = lax.axis_size("tm")
    width = atom_pairs.shape[1]
    row_count = width // devices
    chunk = 512 if devices <= 32 else 128
    gathered = exchange(
        jnp.transpose(positions, (1, 0, 2)), atom_pairs, frame_counts, devices, chunk
    )
    mean_now, mean_lag, cov_now, cov_lag = covariances(*gathered, row_count)
    return (mean_now.reshape(width), mean_lag.reshape(width), cov_now, cov_lag)


def solution(mesh):
    return jax.shard_map(
        body,
        mesh=mesh,
        in_specs=(P(("groups", "tm"), None, None), P(), P("groups")),
        out_specs=(P("groups"), P("groups"), P(("groups", "tm"), None), P(("groups", "tm"), None)),
        check_vma=False,
    )
```

```python
import functools

import jax
import jax.numpy as jnp
from jax import lax
from jax.experimental import pallas as pl
from jax.experimental.pallas import tpu as pltpu
from jax.sharding import PartitionSpec as P

FR = 4
LAG = 1
CORES = 2
PIECES = 2
MIB = 1024 * 1024


def axis_split(devices):
    chips = devices // CORES
    x = 1
    while x * x * x * 8 <= chips and chips % (x * 2) == 0:
        x *= 2
    return chips // x, x


def scoped(devices, wide):
    return (24 if devices <= 32 else wide) * MIB


def split_rows(values):
    parts = []
    for _ in range(PIECES):
        part = values.astype(jnp.bfloat16)
        parts.append(part)
        values = values - part.astype(jnp.float32)
    return parts


def split_into(split_ref, blocks_ref, first):
    frames = split_ref.shape[0] // (3 * PIECES)
    atoms = split_ref.shape[1]
    group = min(frames, 32)

    def split_group(g, carry):
        blocks = blocks_ref[pl.ds(first + g * (group // FR), group // FR)]
        for c in range(3):
            values = blocks[:, c, :, :].reshape(group, atoms)
            for s, part in enumerate(split_rows(values)):
                row = (3 * s + c) * frames + g * group
                if frames != group:
                    row = pl.multiple_of(row, group)
                split_ref[pl.ds(row, group), :] = part
        return carry

    if frames == group:
        split_group(0, 0)
    else:
        lax.fori_loop(0, frames // group, split_group, 0)


def lengths(parts):
    rows = parts.shape[0] // PIECES
    frames = rows // 3
    difference = parts[:rows]
    for s in range(1, PIECES):
        difference = difference + parts[s * rows : (s + 1) * rows]
    squares = difference * difference
    return jnp.sqrt(squares[:frames] + squares[frames : 2 * frames] + squares[2 * frames :])


def distances(split, select):
    return lengths(jnp.dot(split, select, preferred_element_type=jnp.float32))


def ahead_of(rows):
    return jnp.concatenate([rows[LAG:], jnp.zeros((LAG, rows.shape[1]), rows.dtype)], axis=0)


def exchange_kernel(
    sizes,
    own_ref,
    pairs_hbm,
    counts_hbm,
    blocks_ref,
    select_ref,
    half_ref,
    weights_ref,
    pairs_ref,
    counts_ref,
    split_ref,
    load_sem,
    send_sem,
    recv_sem,
    share_sem,
    fetch_sem,
):
    zs, xs = sizes
    me = lax.axis_index("tm")
    core = lax.rem(me, CORES)
    x = lax.rem(me // CORES, xs)
    z = me // (CORES * xs)
    chunks, atoms, width = select_ref.shape
    frames = blocks_ref.shape[0] * FR

    def index(zi, xi, ci):
        return (zi * xs + xi) * CORES + ci

    def device(i):
        return {"tm": i}

    loads = [
        pltpu.make_async_copy(pairs_hbm, pairs_ref, load_sem.at[0]),
        pltpu.make_async_copy(own_ref, blocks_ref.at[me], load_sem.at[1]),
        pltpu.make_async_copy(counts_hbm, counts_ref, load_sem.at[2]),
    ]
    for load in loads:
        load.start()

    sibling = index(z, x, 1 - core)
    x_peers = [lax.rem(x + d, xs) for d in range(1, xs)]
    z_peers = [lax.rem(z + d, zs) for d in range(1, zs) if (zs, d) != (4, 2)]
    barrier = pltpu.get_barrier_semaphore()

    def greet(i):
        pl.semaphore_signal(
            barrier, inc=1, device_id=device(i), device_id_type=pl.DeviceIdType.MESH
        )

    for p in z_peers:
        greet(index(p, x, core))
    for p in x_peers:
        greet(index(z, p, core))
    greet(sibling)

    def build_select(j, carry):
        atom = lax.broadcasted_iota(jnp.int32, (atoms, width), 0).astype(jnp.int16)
        start = pl.multiple_of(j * width, width)
        first = pairs_ref[0:1, pl.ds(start, width)].astype(jnp.int16)
        second = pairs_ref[1:2, pl.ds(start, width)].astype(jnp.int16)
        one, zero = jnp.bfloat16(1.0), jnp.bfloat16(0.0)
        select_ref[j] = jnp.where(atom == first, one, jnp.where(atom == second, -one, zero))
        return carry

    marks = [chunks * p // 16 for p in BUILD]
    done = [0]

    def build_to(mark):
        if mark > done[0]:
            lax.fori_loop(done[0], mark, build_select, 0)
            done[0] = mark

    loads[0].wait()
    build_to(marks[0])
    pl.semaphore_wait(barrier, len(z_peers) + len(x_peers) + 1)

    sent = []

    def send(source, block, target, allowed):
        copy = pltpu.make_async_remote_copy(
            src_ref=source,
            dst_ref=blocks_ref.at[block],
            send_sem=send_sem.at[len(sent)],
            recv_sem=recv_sem.at[block],
            device_id=device(target),
            device_id_type=pl.DeviceIdType.MESH,
        )
        sent.append((copy, allowed))
        if allowed is None:
            copy.start()
        else:
            pl.when(allowed)(copy.start)

    def arrived(block):
        pltpu.make_async_remote_copy(
            src_ref=blocks_ref.at[block],
            dst_ref=blocks_ref.at[block],
            send_sem=send_sem.at[0],
            recv_sem=recv_sem.at[block],
            device_id=device(sibling),
            device_id_type=pl.DeviceIdType.MESH,
        ).wait_recv()

    send(own_ref, me, sibling, None)
    for p in x_peers:
        send(own_ref, me, index(z, p, core), None)
    for d in range(1, zs):
        for sign in (1, -1) if d != 2 else ():
            target = z + sign * d
            exists = target < zs if sign > 0 else target >= 0
            send(own_ref, me, index(target, x, core), exists)

    def origins(d):
        for sign in (-1, 1) if d else (1,):
            origin = z + sign * d
            yield origin, None if d == 0 else (origin >= 0 if sign < 0 else origin < zs)

    def z_event(d):
        for origin, exists in origins(d):
            block = index(origin, x, core)
            pl.when(exists)(functools.partial(arrived, block))
            if d == 1:
                onward = 2 * z - origin
                inside = jnp.logical_and(onward >= 0, onward < zs)
                passed = jnp.logical_and(exists, inside)
                send(blocks_ref.at[block], block, index(onward, x, core), passed)
            send(blocks_ref.at[block], block, sibling, exists)
            for p in x_peers:
                send(blocks_ref.at[block], block, index(z, p, core), exists)

    def x_event(d):
        for origin, exists in origins(d):
            for p in x_peers:
                block = index(origin, p, core)
                if exists is None:
                    arrived(block)
                else:
                    pl.when(exists)(functools.partial(arrived, block))
                send(blocks_ref.at[block], block, sibling, exists)

    near = zs // 2
    level = xs * CORES * FR
    half = z // near
    base = half * near

    build_to(marks[1])
    for loads_left in loads[1:]:
        loads_left.wait()
    frame = lax.broadcasted_iota(jnp.int32, (frames, 128), 0)

    def add_block(b, current):
        return jnp.where(frame // FR == b, counts_ref[b], current)

    current = lax.fori_loop(0, frames // FR, add_block, jnp.zeros((frames, 128), jnp.int32))
    valid = jnp.where(frame % FR < current, 1.0, 0.0)
    weights_ref[...] = valid * ahead_of(valid)
    per_core = chunks // CORES
    first_chunk = core * per_core

    def rows_of(r, p, owner):
        row = pl.multiple_of(lax.rem(z - base + r, near) * level, level)
        part = per_core // 2
        start = owner * per_core + p * part
        return half_ref.at[pl.ds(start, part), pl.ds(row, level), :]

    def share(r, p, owner):
        return pltpu.make_async_remote_copy(
            src_ref=rows_of(r, p, owner),
            dst_ref=rows_of(r, p, owner),
            send_sem=share_sem.at[r, p],
            recv_sem=fetch_sem.at[r, p],
            device_id=device(sibling),
            device_id_type=pl.DeviceIdType.MESH,
        )

    def begin(r):
        zi = base + lax.rem(z - base + r, near)
        for xi in range(xs):
            arrived(index(zi, xi, 1 - core))
        split_into(split_ref, blocks_ref, zi * xs * CORES)

    def featurize(r, start, stop):
        row = pl.multiple_of(lax.rem(z - base + r, near) * level, level)

        def one(i, carry):
            j = first_chunk + i
            half_ref[j, pl.ds(row, level), :] = distances(split_ref[...], select_ref[j])
            return carry

        lax.fori_loop(per_core * start // 8, per_core * stop // 8, one, 0)
        if start < 4 <= stop:
            share(r, 0, core).start()
        if start < 8 == stop:
            share(r, 1, core).start()

    drained = [0]

    def drain(upto):
        for copy, allowed in sent[drained[0] : upto]:
            if allowed is None:
                copy.wait_send()
            else:
                pl.when(allowed)(copy.wait_send)
        drained[0] = upto

    z_event(1)
    x_event(0)
    first_sends = len(sent)
    build_to(chunks)
    begin(0)
    featurize(0, 0, OWN)
    for d in reversed(range(2, zs)):
        z_event(d)
    for d in range(1, near):
        x_event(d)
    featurize(0, OWN, 8)
    for r in range(1, near):
        begin(r)
        featurize(r, 0, OTHER)
        if r == near - 1:
            drain(first_sends)
            for d in range(near, zs):
                x_event(d)
        featurize(r, OTHER, 8)

    for zi in range(near):
        for xi in range(xs):
            arrived(index((1 - half) * near + zi, xi, 1 - core))
    for r in range(near):
        for p in (0, 1):
            share(r, p, core).wait_send()
            share(r, p, 1 - core).wait_recv()
    drain(len(sent))


BUILD = [2, 13, 16]
OWN = 5
OTHER = 8


def exchange(block, atom_pairs, frame_counts, devices, chunk):
    zs, xs = axis_split(devices)
    atoms = block.shape[2]
    frames = devices * FR
    chunks = atom_pairs.shape[1] // chunk
    dma = pltpu.SemaphoreType.DMA
    sends = 2 + (xs - 1) + 2 * (zs - 1) + 1 + 2 * (zs - 1) * xs + (2 * zs - 1) * (xs - 1)
    return pl.pallas_call(
        functools.partial(exchange_kernel, (zs, xs)),
        out_shape=(
            pltpu.VMEM((devices,) + block.shape, jnp.float32),
            pltpu.VMEM((chunks, atoms, chunk), jnp.bfloat16),
            pltpu.VMEM((chunks, frames // 2, chunk), jnp.float32),
            pltpu.VMEM((frames, 128), jnp.float32),
        ),
        in_specs=[pl.BlockSpec(memory_space=pltpu.HBM)] * 3,
        out_specs=(pl.BlockSpec(memory_space=pltpu.VMEM),) * 4,
        scratch_shapes=[
            pltpu.VMEM(atom_pairs.shape, jnp.int32),
            pltpu.SMEM(frame_counts.shape, jnp.int32),
            pltpu.VMEM((3 * PIECES * xs * CORES * FR, atoms), jnp.bfloat16),
            dma((3,)),
            dma((sends,)),
            dma((devices,)),
            dma((zs // 2, 2)),
            dma((zs // 2, 2)),
        ],
        compiler_params=pltpu.CompilerParams(
            collective_id=0, has_side_effects=True, vmem_limit_bytes=scoped(devices, 14)
        ),
        name="exchange",
    )(*(pltpu.with_memory_space_constraint(a, pltpu.HBM) for a in (block, atom_pairs, frame_counts)))


SLOTS = 4


def covariance_kernel(
    row_count,
    blocks_ref,
    select_ref,
    half_ref,
    weights_ref,
    mean_now_ref,
    mean_lag_ref,
    cov_now_ref,
    cov_lag_ref,
    left_ref,
    split_ref,
    parts_ref,
    early_ref,
    late_ref,
    tiles_ref,
    write_sem,
):
    chunks, part, width = half_ref.shape
    me = lax.axis_index("tm")
    held = blocks_ref.shape[0]
    mine = me // (held // 2)
    other = 1 - mine
    first = me * row_count // width

    def widened(rows):
        return jnp.concatenate([rows] * (width // 128), axis=1)

    scale = widened(1.0 / jnp.sum(weights_ref[...], axis=0, keepdims=True))

    def mean_of(rows):
        return jnp.sum(widened(weights_ref[...]) * rows, axis=0, keepdims=True) * scale

    def chunk_of(s):
        return lax.rem(first + s, chunks)

    def project(s):
        parts_ref[lax.rem(s, 2)] = jnp.dot(
            split_ref[...], select_ref[chunk_of(s)], preferred_element_type=jnp.float32
        )

    def center(s):
        j = chunk_of(s)
        slot = lax.rem(s, 2)
        ours = half_ref[j]
        theirs = lengths(parts_ref[slot])
        features = jnp.where(
            mine == 0,
            jnp.concatenate([ours, theirs], axis=0),
            jnp.concatenate([theirs, ours], axis=0),
        )
        ahead = ahead_of(features)
        mean_now = mean_of(features)
        mean_lag = mean_of(ahead)
        column = pl.ds(pl.multiple_of(j * width, width), width)
        mean_now_ref[:, column] = mean_now
        mean_lag_ref[:, column] = mean_lag
        early_ref[slot] = (features - mean_now).astype(jnp.bfloat16)
        late_ref[slot] = (ahead - mean_lag).astype(jnp.bfloat16)

    def writes(s):
        column = pl.multiple_of(chunk_of(s) * width, width)
        at = lax.rem(s, SLOTS)
        return [
            pltpu.make_async_copy(
                tiles_ref.at[at, o], ref.at[:, pl.ds(column, width)], write_sem.at[at, o]
            )
            for o, ref in enumerate((cov_now_ref, cov_lag_ref))
        ]

    def multiply(s):
        slot = lax.rem(s, 2)
        at = lax.rem(s, SLOTS)
        if row_count == width:
            left = left_ref[...]
        else:
            offset = lax.rem(me * row_count, width)
            left = left_ref[pl.ds(pl.multiple_of(offset, row_count), row_count), :]
        n = max(row_count // 4, 16)
        for r in range(0, row_count, n):
            for o, ref in enumerate((early_ref, late_ref)):
                product = jnp.dot(left[r : r + n], ref[slot], preferred_element_type=jnp.float32)
                tiles_ref[at, o, r : r + n] = product * scale

    def finish(s):
        for write in writes(s):
            write.wait()

    split_into(split_ref, blocks_ref, other * (held // 2))
    project(0)
    project(1)
    center(0)
    left = early_ref[0].astype(jnp.float32) * widened(weights_ref[...])
    left_ref[...] = jnp.transpose(left).astype(jnp.bfloat16)

    def step(s, carry):
        pl.when(s >= SLOTS)(lambda: finish(s - SLOTS))
        multiply(s)
        center(s + 1)
        project(s + 2)
        for write in writes(s):
            write.start()
        return carry

    lax.fori_loop(0, chunks - 2, step, 0)
    for s in (chunks - 2, chunks - 1):
        finish(s - SLOTS)
        multiply(s)
        if s == chunks - 2:
            center(s + 1)
        for write in writes(s):
            write.start()
    for s in range(chunks - SLOTS, chunks):
        finish(s)


def covariances(blocks, select, half, weights, row_count):
    chunks, part, chunk = half.shape
    atoms = blocks.shape[3]
    width = chunks * chunk
    row = jax.ShapeDtypeStruct((1, width), jnp.float32)
    matrix = jax.ShapeDtypeStruct((row_count, width), jnp.float32)
    return pl.pallas_call(
        functools.partial(covariance_kernel, row_count),
        out_shape=(row, row, matrix, matrix),
        in_specs=[pl.BlockSpec(memory_space=pltpu.VMEM)] * 4,
        out_specs=(
            pl.BlockSpec(memory_space=pltpu.VMEM),
            pl.BlockSpec(memory_space=pltpu.VMEM),
            pl.BlockSpec(memory_space=pl.ANY),
            pl.BlockSpec(memory_space=pl.ANY),
        ),
        scratch_shapes=[
            pltpu.VMEM((chunk, 2 * part), jnp.bfloat16),
            pltpu.VMEM((3 * PIECES * part, atoms), jnp.bfloat16),
            pltpu.VMEM((2, 3 * PIECES * part, chunk), jnp.float32),
            pltpu.VMEM((2, 2 * part, chunk), jnp.bfloat16),
            pltpu.VMEM((2, 2 * part, chunk), jnp.bfloat16),
            pltpu.VMEM((SLOTS, 2, row_count, chunk), jnp.float32),
            pltpu.SemaphoreType.DMA((SLOTS, 2)),
        ],
        compiler_params=pltpu.CompilerParams(
            vmem_limit_bytes=scoped(blocks.shape[0], 56)
        ),
        name="covariances",
    )(blocks, select, half, weights)


def body(positions, atom_pairs, frame_counts):
    devices = lax.axis_size("tm")
    width = atom_pairs.shape[1]
    row_count = width // devices
    chunk = 512 if devices <= 32 else 128
    gathered = exchange(
        jnp.transpose(positions, (1, 0, 2)), atom_pairs, frame_counts, devices, chunk
    )
    mean_now, mean_lag, cov_now, cov_lag = covariances(*gathered, row_count)
    return (mean_now.reshape(width), mean_lag.reshape(width), cov_now, cov_lag)


def solution(mesh):
    return jax.shard_map(
        body,
        mesh=mesh,
        in_specs=(P(("groups", "tm"), None, None), P(), P("groups")),
        out_specs=(P("groups"), P("groups"), P(("groups", "tm"), None), P(("groups", "tm"), None)),
        check_vma=False,
    )
```

```python
import functools

import jax
import jax.numpy as jnp
from jax import lax
from jax.experimental import pallas as pl
from jax.experimental.pallas import tpu as pltpu
from jax.sharding import PartitionSpec as P

FR = 4
LAG = 1
CORES = 2
PIECES = 2
MIB = 1024 * 1024


def axis_split(devices):
    chips = devices // CORES
    x = 1
    while x * x * x * 8 <= chips and chips % (x * 2) == 0:
        x *= 2
    return chips // x, x


def scoped(devices, wide):
    return (24 if devices <= 32 else wide) * MIB


def split_rows(values):
    parts = []
    for _ in range(PIECES):
        part = values.astype(jnp.bfloat16)
        parts.append(part)
        values = values - part.astype(jnp.float32)
    return parts


def split_into(split_ref, blocks_ref, first):
    frames = split_ref.shape[0] // (3 * PIECES)
    atoms = split_ref.shape[1]
    group = min(frames, 32)

    def split_group(g, carry):
        blocks = blocks_ref[pl.ds(first + g * (group // FR), group // FR)]
        for c in range(3):
            values = blocks[:, c, :, :].reshape(group, atoms)
            for s, part in enumerate(split_rows(values)):
                row = (3 * s + c) * frames + g * group
                if frames != group:
                    row = pl.multiple_of(row, group)
                split_ref[pl.ds(row, group), :] = part
        return carry

    if frames == group:
        split_group(0, 0)
    else:
        lax.fori_loop(0, frames // group, split_group, 0)


def lengths(parts):
    rows = parts.shape[0] // PIECES
    frames = rows // 3
    difference = parts[:rows]
    for s in range(1, PIECES):
        difference = difference + parts[s * rows : (s + 1) * rows]
    squares = difference * difference
    return jnp.sqrt(squares[:frames] + squares[frames : 2 * frames] + squares[2 * frames :])


def distances(split, select):
    return lengths(jnp.dot(split, select, preferred_element_type=jnp.float32))


def ahead_of(rows):
    return jnp.concatenate([rows[LAG:], jnp.zeros((LAG, rows.shape[1]), rows.dtype)], axis=0)


def exchange_kernel(
    sizes,
    own_ref,
    pairs_hbm,
    counts_hbm,
    blocks_ref,
    select_ref,
    half_ref,
    weights_ref,
    pairs_ref,
    counts_ref,
    split_ref,
    load_sem,
    send_sem,
    recv_sem,
    share_sem,
    fetch_sem,
):
    zs, xs = sizes
    me = lax.axis_index("tm")
    core = lax.rem(me, CORES)
    x = lax.rem(me // CORES, xs)
    z = me // (CORES * xs)
    chunks, atoms, width = select_ref.shape
    frames = blocks_ref.shape[0] * FR

    def index(zi, xi, ci):
        return (zi * xs + xi) * CORES + ci

    def device(i):
        return {"tm": i}

    loads = [
        pltpu.make_async_copy(pairs_hbm, pairs_ref, load_sem.at[0]),
        pltpu.make_async_copy(own_ref, blocks_ref.at[me], load_sem.at[1]),
        pltpu.make_async_copy(counts_hbm, counts_ref, load_sem.at[2]),
    ]
    for load in loads:
        load.start()

    sibling = index(z, x, 1 - core)
    x_peers = [lax.rem(x + d, xs) for d in range(1, xs)]
    z_peers = [lax.rem(z + d, zs) for d in range(1, zs) if (zs, d) != (4, 2)]
    barrier = pltpu.get_barrier_semaphore()

    def greet(i):
        pl.semaphore_signal(
            barrier, inc=1, device_id=device(i), device_id_type=pl.DeviceIdType.MESH
        )

    for p in z_peers:
        greet(index(p, x, core))
    for p in x_peers:
        greet(index(z, p, core))
    greet(sibling)

    def build_select(j, carry):
        atom = lax.broadcasted_iota(jnp.int32, (atoms, width), 0).astype(jnp.int16)
        start = pl.multiple_of(j * width, width)
        first = pairs_ref[0:1, pl.ds(start, width)].astype(jnp.int16)
        second = pairs_ref[1:2, pl.ds(start, width)].astype(jnp.int16)
        one, zero = jnp.bfloat16(1.0), jnp.bfloat16(0.0)
        select_ref[j] = jnp.where(atom == first, one, jnp.where(atom == second, -one, zero))
        return carry

    marks = [chunks * p // 16 for p in BUILD]
    done = [0]

    def build_to(mark):
        if mark > done[0]:
            lax.fori_loop(done[0], mark, build_select, 0)
            done[0] = mark

    loads[0].wait()
    build_to(marks[0])
    pl.semaphore_wait(barrier, len(z_peers) + len(x_peers) + 1)

    sent = []

    def send(source, block, target, allowed):
        copy = pltpu.make_async_remote_copy(
            src_ref=source,
            dst_ref=blocks_ref.at[block],
            send_sem=send_sem.at[len(sent)],
            recv_sem=recv_sem.at[block],
            device_id=device(target),
            device_id_type=pl.DeviceIdType.MESH,
        )
        sent.append((copy, allowed))
        if allowed is None:
            copy.start()
        else:
            pl.when(allowed)(copy.start)

    def arrived(block):
        pltpu.make_async_remote_copy(
            src_ref=blocks_ref.at[block],
            dst_ref=blocks_ref.at[block],
            send_sem=send_sem.at[0],
            recv_sem=recv_sem.at[block],
            device_id=device(sibling),
            device_id_type=pl.DeviceIdType.MESH,
        ).wait_recv()

    send(own_ref, me, sibling, None)
    for p in x_peers:
        send(own_ref, me, index(z, p, core), None)
    for d in range(1, zs):
        for sign in (1, -1) if d != 2 else ():
            target = z + sign * d
            exists = target < zs if sign > 0 else target >= 0
            send(own_ref, me, index(target, x, core), exists)

    def origins(d):
        for sign in (-1, 1) if d else (1,):
            origin = z + sign * d
            yield origin, None if d == 0 else (origin >= 0 if sign < 0 else origin < zs)

    def z_event(d):
        for origin, exists in origins(d):
            block = index(origin, x, core)
            pl.when(exists)(functools.partial(arrived, block))
            if d == 1:
                onward = 2 * z - origin
                inside = jnp.logical_and(onward >= 0, onward < zs)
                passed = jnp.logical_and(exists, inside)
                send(blocks_ref.at[block], block, index(onward, x, core), passed)
            send(blocks_ref.at[block], block, sibling, exists)
            for p in x_peers:
                send(blocks_ref.at[block], block, index(z, p, core), exists)

    def x_event(d):
        for origin, exists in origins(d):
            for p in x_peers:
                block = index(origin, p, core)
                if exists is None:
                    arrived(block)
                else:
                    pl.when(exists)(functools.partial(arrived, block))
                send(blocks_ref.at[block], block, sibling, exists)

    near = zs // 2
    level = xs * CORES * FR
    half = z // near
    base = half * near

    build_to(marks[1])
    for loads_left in loads[1:]:
        loads_left.wait()
    frame = lax.broadcasted_iota(jnp.int32, (frames, 128), 0)

    def add_block(b, current):
        return jnp.where(frame // FR == b, counts_ref[b], current)

    current = lax.fori_loop(0, frames // FR, add_block, jnp.zeros((frames, 128), jnp.int32))
    valid = jnp.where(frame % FR < current, 1.0, 0.0)
    weights_ref[...] = valid * ahead_of(valid)
    per_core = chunks // CORES
    first_chunk = core * per_core

    def rows_of(r, p, owner):
        row = pl.multiple_of(lax.rem(z - base + r, near) * level, level)
        part = per_core // 2
        start = owner * per_core + p * part
        return half_ref.at[pl.ds(start, part), pl.ds(row, level), :]

    def share(r, p, owner):
        return pltpu.make_async_remote_copy(
            src_ref=rows_of(r, p, owner),
            dst_ref=rows_of(r, p, owner),
            send_sem=share_sem.at[r, p],
            recv_sem=fetch_sem.at[r, p],
            device_id=device(sibling),
            device_id_type=pl.DeviceIdType.MESH,
        )

    def begin(r):
        zi = base + lax.rem(z - base + r, near)
        for xi in range(xs):
            arrived(index(zi, xi, 1 - core))
        split_into(split_ref, blocks_ref, zi * xs * CORES)

    def featurize(r, start, stop):
        row = pl.multiple_of(lax.rem(z - base + r, near) * level, level)

        def one(i, carry):
            j = first_chunk + i
            half_ref[j, pl.ds(row, level), :] = distances(split_ref[...], select_ref[j])
            return carry

        lax.fori_loop(per_core * start // 8, per_core * stop // 8, one, 0)
        if start < 4 <= stop:
            share(r, 0, core).start()
        if start < 8 == stop:
            share(r, 1, core).start()

    drained = [0]

    def drain(upto):
        for copy, allowed in sent[drained[0] : upto]:
            if allowed is None:
                copy.wait_send()
            else:
                pl.when(allowed)(copy.wait_send)
        drained[0] = upto

    z_event(1)
    x_event(0)
    first_sends = len(sent)
    build_to(chunks)
    begin(0)
    featurize(0, 0, OWN)
    for d in reversed(range(2, zs)):
        z_event(d)
    for d in range(1, near):
        x_event(d)
    featurize(0, OWN, 8)
    for r in range(1, near):
        begin(r)
        featurize(r, 0, OTHER)
        if r == near - 1:
            drain(first_sends)
            for d in range(near, zs):
                x_event(d)
        featurize(r, OTHER, 8)

    for zi in range(near):
        for xi in range(xs):
            arrived(index((1 - half) * near + zi, xi, 1 - core))
    for r in range(near):
        for p in (0, 1):
            share(r, p, core).wait_send()
            share(r, p, 1 - core).wait_recv()
    drain(len(sent))


BUILD = [2, 13, 16]
OWN = 5
OTHER = 8


def exchange(block, atom_pairs, frame_counts, devices, chunk):
    zs, xs = axis_split(devices)
    atoms = block.shape[2]
    frames = devices * FR
    chunks = atom_pairs.shape[1] // chunk
    dma = pltpu.SemaphoreType.DMA
    sends = 2 + (xs - 1) + 2 * (zs - 1) + 1 + 2 * (zs - 1) * xs + (2 * zs - 1) * (xs - 1)
    return pl.pallas_call(
        functools.partial(exchange_kernel, (zs, xs)),
        out_shape=(
            pltpu.VMEM((devices,) + block.shape, jnp.float32),
            pltpu.VMEM((chunks, atoms, chunk), jnp.bfloat16),
            pltpu.VMEM((chunks, frames // 2, chunk), jnp.float32),
            pltpu.VMEM((frames, 128), jnp.float32),
        ),
        in_specs=[pl.BlockSpec(memory_space=pltpu.HBM)] * 3,
        out_specs=(pl.BlockSpec(memory_space=pltpu.VMEM),) * 4,
        scratch_shapes=[
            pltpu.VMEM(atom_pairs.shape, jnp.int32),
            pltpu.SMEM(frame_counts.shape, jnp.int32),
            pltpu.VMEM((3 * PIECES * xs * CORES * FR, atoms), jnp.bfloat16),
            dma((3,)),
            dma((sends,)),
            dma((devices,)),
            dma((zs // 2, 2)),
            dma((zs // 2, 2)),
        ],
        compiler_params=pltpu.CompilerParams(
            collective_id=0, has_side_effects=True, vmem_limit_bytes=scoped(devices, 14)
        ),
        name="exchange",
    )(*(pltpu.with_memory_space_constraint(a, pltpu.HBM) for a in (block, atom_pairs, frame_counts)))


SLOTS = 4


def covariance_kernel(
    row_count,
    blocks_ref,
    select_ref,
    half_ref,
    weights_ref,
    mean_now_ref,
    mean_lag_ref,
    cov_now_ref,
    cov_lag_ref,
    left_ref,
    split_ref,
    parts_ref,
    centered_ref,
    tiles_ref,
    write_sem,
):
    chunks, part, width = half_ref.shape
    me = lax.axis_index("tm")
    held = blocks_ref.shape[0]
    mine = me // (held // 2)
    other = 1 - mine
    first = me * row_count // width

    def widened(rows):
        return jnp.concatenate([rows] * (width // 128), axis=1)

    scale = widened(1.0 / jnp.sum(weights_ref[...], axis=0, keepdims=True))

    def mean_of(rows):
        return jnp.sum(widened(weights_ref[...]) * rows, axis=0, keepdims=True) * scale

    def chunk_of(s):
        return lax.rem(first + s, chunks)

    def project(s):
        parts_ref[lax.rem(s, 2)] = jnp.dot(
            split_ref[...], select_ref[chunk_of(s)], preferred_element_type=jnp.float32
        )

    def center(s):
        j = chunk_of(s)
        slot = lax.rem(s, 2)
        ours = half_ref[j]
        theirs = lengths(parts_ref[slot])
        features = jnp.where(
            mine == 0,
            jnp.concatenate([ours, theirs], axis=0),
            jnp.concatenate([theirs, ours], axis=0),
        )
        ahead = ahead_of(features)
        mean_now = mean_of(features)
        mean_lag = mean_of(ahead)
        column = pl.ds(pl.multiple_of(j * width, width), width)
        mean_now_ref[:, column] = mean_now
        mean_lag_ref[:, column] = mean_lag
        centered_ref[slot, :, :width] = (features - mean_now).astype(jnp.bfloat16)
        centered_ref[slot, :, width:] = (ahead - mean_lag).astype(jnp.bfloat16)

    def writes(s):
        column = pl.multiple_of(chunk_of(s) * width, width)
        at = lax.rem(s, SLOTS)
        return [
            pltpu.make_async_copy(
                tiles_ref.at[at, o], ref.at[:, pl.ds(column, width)], write_sem.at[at, o]
            )
            for o, ref in enumerate((cov_now_ref, cov_lag_ref))
        ]

    def multiply(s):
        slot = lax.rem(s, 2)
        at = lax.rem(s, SLOTS)
        if row_count == width:
            left = left_ref[...]
        else:
            offset = lax.rem(me * row_count, width)
            left = left_ref[pl.ds(pl.multiple_of(offset, row_count), row_count), :]
        n = max(row_count // 4, 16)
        for r in range(0, row_count, n):
            product = jnp.dot(
                left[r : r + n], centered_ref[slot], preferred_element_type=jnp.float32
            )
            tiles_ref[at, 0, r : r + n] = product[:, :width] * scale
            tiles_ref[at, 1, r : r + n] = product[:, width:] * scale

    def finish(s):
        for write in writes(s):
            write.wait()

    split_into(split_ref, blocks_ref, other * (held // 2))
    project(0)
    project(1)
    center(0)
    left = centered_ref[0, :, :width].astype(jnp.float32) * widened(weights_ref[...])
    left_ref[...] = jnp.transpose(left).astype(jnp.bfloat16)

    def step(s, carry):
        pl.when(s >= SLOTS)(lambda: finish(s - SLOTS))
        multiply(s)
        center(s + 1)
        project(s + 2)
        for write in writes(s):
            write.start()
        return carry

    lax.fori_loop(0, chunks - 2, step, 0)
    for s in (chunks - 2, chunks - 1):
        finish(s - SLOTS)
        multiply(s)
        if s == chunks - 2:
            center(s + 1)
        for write in writes(s):
            write.start()
    for s in range(chunks - SLOTS, chunks):
        finish(s)


def covariances(blocks, select, half, weights, row_count):
    chunks, part, chunk = half.shape
    atoms = blocks.shape[3]
    width = chunks * chunk
    row = jax.ShapeDtypeStruct((1, width), jnp.float32)
    matrix = jax.ShapeDtypeStruct((row_count, width), jnp.float32)
    return pl.pallas_call(
        functools.partial(covariance_kernel, row_count),
        out_shape=(row, row, matrix, matrix),
        in_specs=[pl.BlockSpec(memory_space=pltpu.VMEM)] * 4,
        out_specs=(
            pl.BlockSpec(memory_space=pltpu.VMEM),
            pl.BlockSpec(memory_space=pltpu.VMEM),
            pl.BlockSpec(memory_space=pl.ANY),
            pl.BlockSpec(memory_space=pl.ANY),
        ),
        scratch_shapes=[
            pltpu.VMEM((chunk, 2 * part), jnp.bfloat16),
            pltpu.VMEM((3 * PIECES * part, atoms), jnp.bfloat16),
            pltpu.VMEM((2, 3 * PIECES * part, chunk), jnp.float32),
            pltpu.VMEM((2, 2 * part, 2 * chunk), jnp.bfloat16),
            pltpu.VMEM((SLOTS, 2, row_count, chunk), jnp.float32),
            pltpu.SemaphoreType.DMA((SLOTS, 2)),
        ],
        compiler_params=pltpu.CompilerParams(
            vmem_limit_bytes=scoped(blocks.shape[0], 56)
        ),
        name="covariances",
    )(blocks, select, half, weights)


def body(positions, atom_pairs, frame_counts):
    devices = lax.axis_size("tm")
    width = atom_pairs.shape[1]
    row_count = width // devices
    chunk = 512 if devices <= 32 else 128
    gathered = exchange(
        jnp.transpose(positions, (1, 0, 2)), atom_pairs, frame_counts, devices, chunk
    )
    mean_now, mean_lag, cov_now, cov_lag = covariances(*gathered, row_count)
    return (mean_now.reshape(width), mean_lag.reshape(width), cov_now, cov_lag)


def solution(mesh):
    return jax.shard_map(
        body,
        mesh=mesh,
        in_specs=(P(("groups", "tm"), None, None), P(), P("groups")),
        out_specs=(P("groups"), P("groups"), P(("groups", "tm"), None), P(("groups", "tm"), None)),
        check_vma=False,
    )
```

```python
import functools

import jax
import jax.numpy as jnp
from jax import lax
from jax.experimental import pallas as pl
from jax.experimental.pallas import tpu as pltpu
from jax.sharding import PartitionSpec as P

FR = 4
LAG = 1
CORES = 2
PIECES = 2
MIB = 1024 * 1024


def axis_split(devices):
    chips = devices // CORES
    x = 1
    while x * x * x * 8 <= chips and chips % (x * 2) == 0:
        x *= 2
    return chips // x, x


def scoped(devices, wide):
    return (24 if devices <= 32 else wide) * MIB


def split_rows(values):
    parts = []
    for _ in range(PIECES):
        part = values.astype(jnp.bfloat16)
        parts.append(part)
        values = values - part.astype(jnp.float32)
    return parts


def split_into(split_ref, blocks_ref, first):
    frames = split_ref.shape[0] // (3 * PIECES)
    atoms = split_ref.shape[1]
    group = min(frames, 32)

    def split_group(g, carry):
        blocks = blocks_ref[pl.ds(first + g * (group // FR), group // FR)]
        for c in range(3):
            values = blocks[:, c, :, :].reshape(group, atoms)
            for s, part in enumerate(split_rows(values)):
                row = (3 * s + c) * frames + g * group
                if frames != group:
                    row = pl.multiple_of(row, group)
                split_ref[pl.ds(row, group), :] = part
        return carry

    if frames == group:
        split_group(0, 0)
    else:
        lax.fori_loop(0, frames // group, split_group, 0)


def lengths(parts):
    rows = parts.shape[0] // PIECES
    frames = rows // 3
    difference = parts[:rows]
    for s in range(1, PIECES):
        difference = difference + parts[s * rows : (s + 1) * rows]
    squares = difference * difference
    return jnp.sqrt(squares[:frames] + squares[frames : 2 * frames] + squares[2 * frames :])


def distances(split, select):
    return lengths(jnp.dot(split, select, preferred_element_type=jnp.float32))


def ahead_of(rows):
    return jnp.concatenate([rows[LAG:], jnp.zeros((LAG, rows.shape[1]), rows.dtype)], axis=0)


def exchange_kernel(
    sizes,
    own_ref,
    pairs_hbm,
    counts_hbm,
    blocks_ref,
    select_ref,
    half_ref,
    weights_ref,
    pairs_ref,
    counts_ref,
    split_ref,
    load_sem,
    send_sem,
    recv_sem,
    share_sem,
    fetch_sem,
):
    zs, xs = sizes
    me = lax.axis_index("tm")
    core = lax.rem(me, CORES)
    x = lax.rem(me // CORES, xs)
    z = me // (CORES * xs)
    chunks, atoms, width = select_ref.shape
    frames = blocks_ref.shape[0] * FR

    def index(zi, xi, ci):
        return (zi * xs + xi) * CORES + ci

    def device(i):
        return {"tm": i}

    loads = [
        pltpu.make_async_copy(pairs_hbm, pairs_ref, load_sem.at[0]),
        pltpu.make_async_copy(own_ref, blocks_ref.at[me], load_sem.at[1]),
        pltpu.make_async_copy(counts_hbm, counts_ref, load_sem.at[2]),
    ]
    for load in loads:
        load.start()

    sibling = index(z, x, 1 - core)
    x_peers = [lax.rem(x + d, xs) for d in range(1, xs)]
    z_peers = [lax.rem(z + d, zs) for d in range(1, zs) if (zs, d) != (4, 2)]
    barrier = pltpu.get_barrier_semaphore()

    def greet(i):
        pl.semaphore_signal(
            barrier, inc=1, device_id=device(i), device_id_type=pl.DeviceIdType.MESH
        )

    for p in z_peers:
        greet(index(p, x, core))
    for p in x_peers:
        greet(index(z, p, core))
    greet(sibling)

    def build_select(j, carry):
        atom = lax.broadcasted_iota(jnp.int32, (atoms, width), 0).astype(jnp.int16)
        start = pl.multiple_of(j * width, width)
        first = pairs_ref[0:1, pl.ds(start, width)].astype(jnp.int16)
        second = pairs_ref[1:2, pl.ds(start, width)].astype(jnp.int16)
        one, zero = jnp.bfloat16(1.0), jnp.bfloat16(0.0)
        select_ref[j] = jnp.where(atom == first, one, jnp.where(atom == second, -one, zero))
        return carry

    marks = [chunks * p // 16 for p in BUILD]
    done = [0]

    def build_to(mark):
        if mark > done[0]:
            lax.fori_loop(done[0], mark, build_select, 0)
            done[0] = mark

    loads[0].wait()
    build_to(marks[0])
    pl.semaphore_wait(barrier, len(z_peers) + len(x_peers) + 1)

    sent = []

    def send(source, block, target, allowed):
        copy = pltpu.make_async_remote_copy(
            src_ref=source,
            dst_ref=blocks_ref.at[block],
            send_sem=send_sem.at[len(sent)],
            recv_sem=recv_sem.at[block],
            device_id=device(target),
            device_id_type=pl.DeviceIdType.MESH,
        )
        sent.append((copy, allowed))
        if allowed is None:
            copy.start()
        else:
            pl.when(allowed)(copy.start)

    def arrived(block):
        pltpu.make_async_remote_copy(
            src_ref=blocks_ref.at[block],
            dst_ref=blocks_ref.at[block],
            send_sem=send_sem.at[0],
            recv_sem=recv_sem.at[block],
            device_id=device(sibling),
            device_id_type=pl.DeviceIdType.MESH,
        ).wait_recv()

    send(own_ref, me, sibling, None)
    for p in x_peers:
        send(own_ref, me, index(z, p, core), None)
    for d in range(1, zs):
        for sign in (1, -1) if d != 2 else ():
            target = z + sign * d
            exists = target < zs if sign > 0 else target >= 0
            send(own_ref, me, index(target, x, core), exists)

    def origins(d):
        for sign in (-1, 1) if d else (1,):
            origin = z + sign * d
            yield origin, None if d == 0 else (origin >= 0 if sign < 0 else origin < zs)

    def z_event(d):
        for origin, exists in origins(d):
            block = index(origin, x, core)
            pl.when(exists)(functools.partial(arrived, block))
            if d == 1:
                onward = 2 * z - origin
                inside = jnp.logical_and(onward >= 0, onward < zs)
                passed = jnp.logical_and(exists, inside)
                send(blocks_ref.at[block], block, index(onward, x, core), passed)
            send(blocks_ref.at[block], block, sibling, exists)
            for p in x_peers:
                send(blocks_ref.at[block], block, index(z, p, core), exists)

    def x_event(d):
        for origin, exists in origins(d):
            for p in x_peers:
                block = index(origin, p, core)
                if exists is None:
                    arrived(block)
                else:
                    pl.when(exists)(functools.partial(arrived, block))
                send(blocks_ref.at[block], block, sibling, exists)

    near = zs // 2
    level = xs * CORES * FR
    half = z // near
    base = half * near

    build_to(marks[1])
    for loads_left in loads[1:]:
        loads_left.wait()
    frame = lax.broadcasted_iota(jnp.int32, (frames, 128), 0)

    def add_block(b, current):
        return jnp.where(frame // FR == b, counts_ref[b], current)

    current = lax.fori_loop(0, frames // FR, add_block, jnp.zeros((frames, 128), jnp.int32))
    valid = jnp.where(frame % FR < current, 1.0, 0.0)
    weights_ref[...] = valid * ahead_of(valid)
    per_core = chunks // CORES
    first_chunk = core * per_core

    def rows_of(r, p, owner):
        row = pl.multiple_of(lax.rem(z - base + r, near) * level, level)
        part = per_core // 2
        start = owner * per_core + p * part
        return half_ref.at[pl.ds(start, part), pl.ds(row, level), :]

    def share(r, p, owner):
        return pltpu.make_async_remote_copy(
            src_ref=rows_of(r, p, owner),
            dst_ref=rows_of(r, p, owner),
            send_sem=share_sem.at[r, p],
            recv_sem=fetch_sem.at[r, p],
            device_id=device(sibling),
            device_id_type=pl.DeviceIdType.MESH,
        )

    def begin(r):
        zi = base + lax.rem(z - base + r, near)
        for xi in range(xs):
            arrived(index(zi, xi, 1 - core))
        split_into(split_ref, blocks_ref, zi * xs * CORES)

    def featurize(r, start, stop):
        row = pl.multiple_of(lax.rem(z - base + r, near) * level, level)

        def one(i, carry):
            j = first_chunk + i
            half_ref[j, pl.ds(row, level), :] = distances(split_ref[...], select_ref[j])
            return carry

        lax.fori_loop(per_core * start // 8, per_core * stop // 8, one, 0)
        if start < 4 <= stop:
            share(r, 0, core).start()
        if start < 8 == stop:
            share(r, 1, core).start()

    drained = [0]

    def drain(upto):
        for copy, allowed in sent[drained[0] : upto]:
            if allowed is None:
                copy.wait_send()
            else:
                pl.when(allowed)(copy.wait_send)
        drained[0] = upto

    z_event(1)
    x_event(0)
    first_sends = len(sent)
    build_to(chunks)
    begin(0)
    featurize(0, 0, OWN)
    for d in reversed(range(3, zs)):
        z_event(d)
    for d in range(1, near):
        x_event(d)
        if d == 1:
            z_event(2)
    featurize(0, OWN, 8)
    for r in range(1, near):
        begin(r)
        featurize(r, 0, OTHER)
        if r == near - 1:
            drain(first_sends)
            for d in range(near, zs):
                x_event(d)
        featurize(r, OTHER, 8)

    for zi in range(near):
        for xi in range(xs):
            arrived(index((1 - half) * near + zi, xi, 1 - core))
    for r in range(near):
        for p in (0, 1):
            share(r, p, core).wait_send()
            share(r, p, 1 - core).wait_recv()
    drain(len(sent))


BUILD = [2, 13, 16]
OWN = 5
OTHER = 8


def exchange(block, atom_pairs, frame_counts, devices, chunk):
    zs, xs = axis_split(devices)
    atoms = block.shape[2]
    frames = devices * FR
    chunks = atom_pairs.shape[1] // chunk
    dma = pltpu.SemaphoreType.DMA
    sends = 2 + (xs - 1) + 2 * (zs - 1) + 1 + 2 * (zs - 1) * xs + (2 * zs - 1) * (xs - 1)
    return pl.pallas_call(
        functools.partial(exchange_kernel, (zs, xs)),
        out_shape=(
            pltpu.VMEM((devices,) + block.shape, jnp.float32),
            pltpu.VMEM((chunks, atoms, chunk), jnp.bfloat16),
            pltpu.VMEM((chunks, frames // 2, chunk), jnp.float32),
            pltpu.VMEM((frames, 128), jnp.float32),
        ),
        in_specs=[pl.BlockSpec(memory_space=pltpu.HBM)] * 3,
        out_specs=(pl.BlockSpec(memory_space=pltpu.VMEM),) * 4,
        scratch_shapes=[
            pltpu.VMEM(atom_pairs.shape, jnp.int32),
            pltpu.SMEM(frame_counts.shape, jnp.int32),
            pltpu.VMEM((3 * PIECES * xs * CORES * FR, atoms), jnp.bfloat16),
            dma((3,)),
            dma((sends,)),
            dma((devices,)),
            dma((zs // 2, 2)),
            dma((zs // 2, 2)),
        ],
        compiler_params=pltpu.CompilerParams(
            collective_id=0, has_side_effects=True, vmem_limit_bytes=scoped(devices, 14)
        ),
        name="exchange",
    )(*(pltpu.with_memory_space_constraint(a, pltpu.HBM) for a in (block, atom_pairs, frame_counts)))


SLOTS = 4


def covariance_kernel(
    row_count,
    blocks_ref,
    select_ref,
    half_ref,
    weights_ref,
    mean_now_ref,
    mean_lag_ref,
    cov_now_ref,
    cov_lag_ref,
    left_ref,
    split_ref,
    parts_ref,
    early_ref,
    late_ref,
    tiles_ref,
    write_sem,
):
    chunks, part, width = half_ref.shape
    me = lax.axis_index("tm")
    held = blocks_ref.shape[0]
    mine = me // (held // 2)
    other = 1 - mine
    first = me * row_count // width

    def widened(rows):
        return jnp.concatenate([rows] * (width // 128), axis=1)

    scale = widened(1.0 / jnp.sum(weights_ref[...], axis=0, keepdims=True))

    def mean_of(rows):
        return jnp.sum(widened(weights_ref[...]) * rows, axis=0, keepdims=True) * scale

    def chunk_of(s):
        return lax.rem(first + s, chunks)

    def project(s):
        parts_ref[lax.rem(s, 2)] = jnp.dot(
            split_ref[...], select_ref[chunk_of(s)], preferred_element_type=jnp.float32
        )

    def center(s):
        j = chunk_of(s)
        slot = lax.rem(s, 2)
        ours = half_ref[j]
        theirs = lengths(parts_ref[slot])
        features = jnp.where(
            mine == 0,
            jnp.concatenate([ours, theirs], axis=0),
            jnp.concatenate([theirs, ours], axis=0),
        )
        ahead = ahead_of(features)
        mean_now = mean_of(features)
        mean_lag = mean_of(ahead)
        column = pl.ds(pl.multiple_of(j * width, width), width)
        mean_now_ref[:, column] = mean_now
        mean_lag_ref[:, column] = mean_lag
        early_ref[slot] = (features - mean_now).astype(jnp.bfloat16)
        late_ref[slot] = (ahead - mean_lag).astype(jnp.bfloat16)

    def writes(s):
        column = pl.multiple_of(chunk_of(s) * width, width)
        at = lax.rem(s, SLOTS)
        return [
            pltpu.make_async_copy(
                tiles_ref.at[at, o], ref.at[:, pl.ds(column, width)], write_sem.at[at, o]
            )
            for o, ref in enumerate((cov_now_ref, cov_lag_ref))
        ]

    def multiply(s):
        slot = lax.rem(s, 2)
        at = lax.rem(s, SLOTS)
        if row_count == width:
            left = left_ref[...]
        else:
            offset = lax.rem(me * row_count, width)
            left = left_ref[pl.ds(pl.multiple_of(offset, row_count), row_count), :]
        n = max(row_count // 4, 16)
        for r in range(0, row_count, n):
            for o, ref in enumerate((early_ref, late_ref)):
                product = jnp.dot(left[r : r + n], ref[slot], preferred_element_type=jnp.float32)
                tiles_ref[at, o, r : r + n] = product * scale

    def finish(s):
        for write in writes(s):
            write.wait()

    split_into(split_ref, blocks_ref, other * (held // 2))
    project(0)
    project(1)
    center(0)
    left = early_ref[0].astype(jnp.float32) * widened(weights_ref[...])
    left_ref[...] = jnp.transpose(left).astype(jnp.bfloat16)

    def step(s, carry):
        pl.when(s >= SLOTS)(lambda: finish(s - SLOTS))
        multiply(s)
        center(s + 1)
        project(s + 2)
        for write in writes(s):
            write.start()
        return carry

    lax.fori_loop(0, chunks - 2, step, 0)
    for s in (chunks - 2, chunks - 1):
        finish(s - SLOTS)
        multiply(s)
        if s == chunks - 2:
            center(s + 1)
        for write in writes(s):
            write.start()
    for s in range(chunks - SLOTS, chunks):
        finish(s)


def covariances(blocks, select, half, weights, row_count):
    chunks, part, chunk = half.shape
    atoms = blocks.shape[3]
    width = chunks * chunk
    row = jax.ShapeDtypeStruct((1, width), jnp.float32)
    matrix = jax.ShapeDtypeStruct((row_count, width), jnp.float32)
    return pl.pallas_call(
        functools.partial(covariance_kernel, row_count),
        out_shape=(row, row, matrix, matrix),
        in_specs=[pl.BlockSpec(memory_space=pltpu.VMEM)] * 4,
        out_specs=(
            pl.BlockSpec(memory_space=pltpu.VMEM),
            pl.BlockSpec(memory_space=pltpu.VMEM),
            pl.BlockSpec(memory_space=pl.ANY),
            pl.BlockSpec(memory_space=pl.ANY),
        ),
        scratch_shapes=[
            pltpu.VMEM((chunk, 2 * part), jnp.bfloat16),
            pltpu.VMEM((3 * PIECES * part, atoms), jnp.bfloat16),
            pltpu.VMEM((2, 3 * PIECES * part, chunk), jnp.float32),
            pltpu.VMEM((2, 2 * part, chunk), jnp.bfloat16),
            pltpu.VMEM((2, 2 * part, chunk), jnp.bfloat16),
            pltpu.VMEM((SLOTS, 2, row_count, chunk), jnp.float32),
            pltpu.SemaphoreType.DMA((SLOTS, 2)),
        ],
        compiler_params=pltpu.CompilerParams(
            vmem_limit_bytes=scoped(blocks.shape[0], 56)
        ),
        name="covariances",
    )(blocks, select, half, weights)


def body(positions, atom_pairs, frame_counts):
    devices = lax.axis_size("tm")
    width = atom_pairs.shape[1]
    row_count = width // devices
    chunk = 512 if devices <= 32 else 128
    gathered = exchange(
        jnp.transpose(positions, (1, 0, 2)), atom_pairs, frame_counts, devices, chunk
    )
    mean_now, mean_lag, cov_now, cov_lag = covariances(*gathered, row_count)
    return (mean_now.reshape(width), mean_lag.reshape(width), cov_now, cov_lag)


def solution(mesh):
    return jax.shard_map(
        body,
        mesh=mesh,
        in_specs=(P(("groups", "tm"), None, None), P(), P("groups")),
        out_specs=(P("groups"), P("groups"), P(("groups", "tm"), None), P(("groups", "tm"), None)),
        check_vma=False,
    )
```
